128 devices in a mesh: dp: 8 (over z, core), dom: 16 (over y, x).
Axes of the slice: x: 4, y: 4, z: 4, core: 2. Of those that a mesh axis runs over, the one named last changes fastest.
Arguments:
- grad_out: bfloat16 [8, 48, 512, 256], P('dp', 'dom'), may hold values from -6 to 6
- pre_act: bfloat16 [8, 48, 512, 256], P('dp', 'dom'), may hold values from -6 to 6
- conv_weight: bfloat16 [27, 256, 256], replicated, may hold values from -0.078125 to 0.078125
- down_weight: bfloat16 [8, 128, 256], replicated, may hold values from -0.1875 to 0.1875
- fine_act: bfloat16 [8, 384, 512, 128], P('dp', 'dom'), may hold values from -6 to 6
- neighbours: int32 [8, 48, 27], P('dp', 'dom'), may hold values from -1 to 2, as said below
- octant_routes: int32 [8, 16, 3, 8], P('dp', 'dom'), may hold values from -1 to 23, as said below
Outputs:
- fine_grad: bfloat16 [8, 384, 512, 128], P('dp', 'dom')
- conv_weight_grad: float32 [6912, 256], P('dp')
- down_weight_grad: float32 [1024, 256], P('dp')
The draws below stay inside these ranges and needn't reach their ends.
Inputs may be any that keep to these rules, and one draw needn't show every extreme that they name: `neighbours`: each device of a scene group has between half of 3 (rounded up) and 3 live slots, always the first ones, and some device of each scene group has all 3 live. A live slot's entry 13 is itself; entry 9(a+1)+3(b+1)+(c+1) is the slot, on the device a steps along dom, of the block displaced by (a, b, c) block edges within a slab of 3 x 3 positions, or -1 where that block is empty or outside the scene group; dead slots hold -1 in all 27 entries; the relation is symmetric. `octant_routes`: row (d, k) lists what device d sends to the device d + k - 1 along dom, taken cyclically: entries 8 s + o name octant o of slot s; each live slot's 8 octants stand together, in order, in exactly one row; live entries come first, then -1. A row holds at most 8 entries, and some row of the fullest device holds exactly 8. Dead slots are never named.
All inputs are finite; a program needn't handle non-finite values.
Results may differ from the reference program's by a relative error of at most 0.0065.
Values may be sent and summed in bfloat16 or wider, within the bound.
A program may use at most 128 MiB of HBM per device.

```python
import math
import jax
import jax.numpy as jnp
from jax import lax

C = 256
CF = 128
BE = 8
GRID_Y = 3
GRID_Z = 3
CAP = 3
PEER = 8
FSLOT = 24
VOX = 512
OCT = 64
SCENES = 8
BLOCKS = 48
FINE = 384
N_DOM = 16


def geometry(key):
    base = jax.random.fold_in(key, 17)
    streams = jax.random.split(base, 4)
    lowest = (CAP + 1) // 2
    counts = jax.random.randint(streams[0], (SCENES, N_DOM), lowest, CAP + 1)
    fullest = jax.random.randint(streams[1], (SCENES, 1), 0, N_DOM)
    counts = jnp.where(jnp.arange(N_DOM)[None, :] == fullest, CAP, counts)
    places = GRID_Y * GRID_Z
    scores = jax.random.randint(streams[2], (SCENES, N_DOM, places), 0, 1 << 20) * places + jnp.arange(places)[None, None, :]
    order = jnp.argsort(scores, axis=-1, stable=True)[..., :CAP].astype(jnp.int32)
    slot_ids = jnp.arange(CAP, dtype=jnp.int32)
    live = slot_ids[None, None, :] < counts[..., None]
    match = (order[..., None] == jnp.arange(places)[None, None, None, :]) & live[..., None]
    occupant = jnp.max(jnp.where(match, slot_ids[None, None, :, None], -1), axis=2).astype(jnp.int32)
    return (order, live, occupant, streams[3])


def draw_neighbours(key, part):
    order, live, occupant, spare = geometry(key)
    places = GRID_Y * GRID_Z
    pos_y = order // GRID_Z
    pos_z = order % GRID_Z
    device = jnp.zeros_like(order) + jnp.arange(N_DOM, dtype=jnp.int32)[None, :, None]
    flat_occupant = occupant.reshape(SCENES, N_DOM * places)
    entries = []
    for step_x in (-1, 0, 1):
        for step_y in (-1, 0, 1):
            for step_z in (-1, 0, 1):
                near_d = device + step_x
                near_y = pos_y + step_y
                near_z = pos_z + step_z
                valid = (near_d >= 0) & (near_d < N_DOM) & (near_y >= 0) & (near_y < GRID_Y) & (near_z >= 0) & (near_z < GRID_Z) & live
                flat = jnp.clip(near_d, 0, N_DOM - 1) * places + jnp.clip(near_y, 0, GRID_Y - 1) * GRID_Z + jnp.clip(near_z, 0, GRID_Z - 1)
                found = jnp.take_along_axis(flat_occupant, flat.reshape(SCENES, -1), axis=1).reshape(flat.shape)
                entries.append(jnp.where(valid, found, -1))
    stacked = jnp.stack(entries, axis=-1).astype(jnp.int32)
    return stacked.reshape(SCENES, N_DOM * CAP, 27)


def draw_octant_routes(key, part):
    order, live, occupant, spare = geometry(key)
    rotate = jax.random.randint(spare, (SCENES, N_DOM, 1), 0, 3)
    slot_ids = jnp.arange(CAP, dtype=jnp.int32)
    heading = (slot_ids[None, None, :] + rotate) % 3
    earlier = (heading[..., :, None] == heading[..., None, :]) & live[..., None, :] & (slot_ids[None, :] < slot_ids[:, None])[None, None]
    rank = jnp.sum(earlier.astype(jnp.int32), axis=-1)
    eighth = jnp.arange(8, dtype=jnp.int32)
    target = rank[..., None] * 8 + eighth
    value = slot_ids[:, None] * 8 + eighth[None, :]
    headings = jnp.arange(3, dtype=jnp.int32)
    places = jnp.arange(PEER, dtype=jnp.int32)
    hit = (heading[:, :, None, None, :, None] == headings[None, None, :, None, None, None]) & (target[:, :, None, None, :, :] == places[None, None, None, :, None, None]) & live[:, :, None, None, :, None]
    routes = jnp.max(jnp.where(hit, value[None, None, None, None], -1), axis=(-2, -1))
    return routes.astype(jnp.int32)


def block_levels(key, extent, cuts, least, largest):
    def one(dim, blocks):
        draws = jax.random.uniform(jax.random.fold_in(jax.random.fold_in(key, 6), dim), (blocks,), jnp.float32, least / len(cuts), largest / len(cuts))
        return jnp.repeat(jnp.exp(draws), extent[dim] // blocks).reshape((-1,) + (1,) * (len(extent) - dim - 1))

    gain = one(*cuts[0])
    for cut in cuts[1:]:
        gain = gain * one(*cut)
    return gain


def normal_values(key, dims, spread, limit, cuts=(), kind=jnp.bfloat16):
    values = jax.random.normal(key, dims, jnp.float32) * spread
    if len(cuts) > 0:
        values = block_levels(key, dims, cuts, -0.22, 0.18) * values
    return jnp.clip(values, min=-limit, max=limit).astype(kind)


def setup_inputs(seed: int = 0) -> dict:
    splits = jax.random.split(jax.random.key(seed), 8)
    grad_out = normal_values(splits[0], (SCENES, BLOCKS, VOX, C), 1.0, 6.0, ((0, 8), (1, 16)))
    pre_act = normal_values(splits[1], (SCENES, BLOCKS, VOX, C), 1.0, 6.0, ((0, 8), (1, 16)))
    conv_weight = normal_values(splits[2], (27, C, C), (27 * C) ** -0.5, 0.078125)
    down_weight = normal_values(splits[3], (8, CF, C), (8 * CF) ** -0.5, 0.1875)
    fine_act = normal_values(splits[4], (SCENES, FINE, VOX, CF), 1.0, 6.0, ((0, 8), (1, 16)))
    neighbours = draw_neighbours(jax.random.fold_in(splits[7], 71), 0)
    octant_routes = draw_octant_routes(jax.random.fold_in(splits[7], 71), 0)
    return {"grad_out": grad_out, "pre_act": pre_act, "conv_weight": conv_weight, "down_weight": down_weight, "fine_act": fine_act, "neighbours": neighbours, "octant_routes": octant_routes}


def pick_rows(source, slot_index):
    extended = jnp.concatenate([source, jnp.zeros_like(source[:1])], axis=0)
    return extended[jnp.where(slot_index < 0, source.shape[0], slot_index).astype(jnp.int32)]

def assemble(own_blocks, lower_faces, upper_faces, block_links):
    block_edge = own_blocks.shape[1]
    sources = (lower_faces, own_blocks, upper_faces)
    ranges = ((block_edge - 1, block_edge), (0, block_edge), (0, 1))
    parts_x = []
    for shift_x in range(3):
        parts_y = []
        for shift_y in range(3):
            parts_z = []
            for shift_z in range(3):
                portion = pick_rows(sources[shift_x], block_links[:, 9 * shift_x + 3 * shift_y + shift_z])
                portion = portion[:, :, ranges[shift_y][0]:ranges[shift_y][1], ranges[shift_z][0]:ranges[shift_z][1]]
                parts_z.append(portion)
            parts_y.append(jnp.concatenate(parts_z, axis=3))
        parts_x.append(jnp.concatenate(parts_y, axis=2))
    return jnp.concatenate(parts_x, axis=1)

def correlate(grad_pad, act_pad, weight):
    block_edge = grad_pad.shape[1] - 2
    channels = grad_pad.shape[-1]

    def window(padded, start_x, start_y, start_z):
        return padded[:, start_x:start_x + block_edge, start_y:start_y + block_edge, start_z:start_z + block_edge].reshape(-1, channels)
    centre_grad = window(grad_pad, 1, 1, 1)
    input_grad = jnp.zeros((centre_grad.shape[0], weight.shape[1]), jnp.float32)
    weight_grads = []
    for position in range(27):
        tap_x = position // 9 - 1
        tap_y = position // 3 % 3 - 1
        tap_z = position % 3 - 1
        input_grad = input_grad + jnp.dot(window(grad_pad, 1 - tap_x, 1 - tap_y, 1 - tap_z), weight[position].T, preferred_element_type=jnp.float32)
        weight_grads.append(jnp.dot(window(act_pad, 1 + tap_x, 1 + tap_y, 1 + tap_z).T, centre_grad, preferred_element_type=jnp.float32))
    return (input_grad, jnp.stack(weight_grads))

def split_octants(blocks):
    count_blocks = blocks.shape[0]
    half_edge = blocks.shape[1] // 2
    channels = blocks.shape[-1]
    parted = blocks.reshape(count_blocks, 2, half_edge, 2, half_edge, 2, half_edge, channels)
    parted = parted.transpose(0, 1, 3, 5, 2, 4, 6, 7)
    return parted.reshape(count_blocks * 8, half_edge * half_edge * half_edge, channels)

def reference(grad_out, pre_act, conv_weight, down_weight, fine_act, neighbours, octant_routes):

    def faces(blocks):
        zero_face = jnp.zeros_like(blocks[:1, :, :1])
        lower = jnp.concatenate([zero_face, blocks[:-1, :, BE - 1:BE]], axis=0)
        upper = jnp.concatenate([blocks[1:, :, 0:1], zero_face], axis=0)
        return (lower, upper)

    def scene(items):
        grad_scene, pre_scene, link_scene, route_scene, fine_scene = items
        grad_blocks = grad_scene.reshape(N_DOM, CAP, BE, BE, BE, C)
        act_blocks = jnp.maximum(pre_scene, 0).reshape(N_DOM, CAP, BE, BE, BE, C)
        block_links = link_scene.reshape(N_DOM, CAP, 27)
        lower_grad, upper_grad = faces(grad_blocks)
        lower_act, upper_act = faces(act_blocks)
        grad_pad = jax.vmap(assemble)(grad_blocks, lower_grad, upper_grad, block_links)
        act_pad = jax.vmap(assemble)(act_blocks, lower_act, upper_act, block_links)
        grad_pad = grad_pad.reshape((N_DOM * CAP,) + grad_pad.shape[2:])
        act_pad = act_pad.reshape((N_DOM * CAP,) + act_pad.shape[2:])
        input_grad, conv_part = correlate(grad_pad, act_pad, conv_weight)
        grad_in = jnp.where(pre_scene.reshape(-1, C) > 0, input_grad, 0.0).astype(jnp.bfloat16)
        octants = split_octants(grad_in.reshape(N_DOM * CAP, BE, BE, BE, C))
        receivers = jnp.arange(N_DOM, dtype=jnp.int32)[:, None]
        headings = jnp.arange(3, dtype=jnp.int32)[None, :]
        senders = ((receivers - headings + 1 + N_DOM) % N_DOM).astype(jnp.int32)
        entries = route_scene[senders, headings]
        flat = jnp.where(entries < 0, -1, senders[..., None] * (CAP * 8) + entries).astype(jnp.int32)
        octant_grad = pick_rows(octants, flat.reshape(-1)).reshape(N_DOM * FSLOT, OCT, C)
        fine_split = fine_scene.reshape(N_DOM * FSLOT, 8, OCT, CF)
        fine_grad = jnp.einsum('fcj,qij->fqci', octant_grad.astype(jnp.float32), down_weight.astype(jnp.float32), precision=lax.Precision.HIGHEST)
        fine_grad = fine_grad.astype(jnp.bfloat16).reshape(N_DOM * FSLOT, VOX, CF)
        down_part = jnp.einsum('fqci,fcj->qij', fine_split.astype(jnp.float32), octant_grad.astype(jnp.float32), precision=lax.Precision.HIGHEST)
        return (fine_grad, conv_part, down_part)
    fine_grad, conv_parts, down_parts = lax.map(scene, (grad_out, pre_act, neighbours, octant_routes, fine_act))
    factor = 1.0 / math.sqrt(SCENES * BLOCKS * VOX)
    conv_total = lax.optimization_barrier(jnp.sum(conv_parts, axis=0)).reshape(27 * C, C) * factor
    down_total = lax.optimization_barrier(jnp.sum(down_parts, axis=0)).reshape(8 * CF, C) * factor
    return (fine_grad, conv_total, down_total)
```

```python
import math

import jax
import jax.numpy as jnp
from jax import lax
from jax.experimental import pallas as pl
from jax.experimental.pallas import tpu as pltpu
from jax.sharding import PartitionSpec as P

MESH = pl.DeviceIdType.MESH
BF = jnp.bfloat16
F32 = jnp.float32
CAP = 3
GROUPS = 4
ORDERS = ("zxy", "xyz", "yzx", "xyz")


def dot_nt(a, b):
    return lax.dot_general(a, b, (((1,), (1,)), ((), ())), preferred_element_type=F32)


def dot_nn(a, b):
    return lax.dot_general(a, b, (((1,), (0,)), ((), ())), preferred_element_type=F32)


def kernel(
    links, routes, g_hbm, p_hbm, w_hbm, dw_hbm, fine_hbm,
    fg_hbm, red_hbm,
    g, p, face, gsh, ash, gt, w, dw, fine, fg, acc, octs, out, octin, ot,
    part, rcore, racc, r1, a1, r2, a2, r3, red,
    load_sem, halo_s, halo_r, oct_s, oct_r, red_s, red_r, fg_sem,
):
    dp = lax.axis_index("dp")
    dom = lax.axis_index("dom")
    zc, cc = dp // 2, dp % 2
    yc, xc = dom // 4, dom % 4
    coord = {"z": zc, "x": xc, "y": yc}

    def dev(axis, to):
        if axis == "z":
            return (to * 2 + cc, dom)
        if axis == "x":
            return (dp, yc * 4 + to)
        return (dp, to * 4 + xc)

    def ring(axis, off):
        return lax.rem(coord[axis] + off, 4)

    partner = (zc * 2 + (1 - cc), dom)
    nxt = (dp, lax.rem(dom + 1, 16))
    prv = (dp, lax.rem(dom + 15, 16))

    barrier = pltpu.get_barrier_semaphore()
    peers = [partner, nxt, prv]
    for axis in "xyz":
        for off in (1, 2, 3):
            peers.append(dev(axis, ring(axis, off)))
    for peer in peers:
        pl.semaphore_signal(barrier, inc=1, device_id=peer, device_id_type=MESH)

    loads = []
    for i, (src, dst) in enumerate(
        ((g_hbm, g.at[0:CAP]), (p_hbm, p.at[0:CAP]), (w_hbm, w), (fine_hbm, fine), (dw_hbm, dw))
    ):
        c = pltpu.make_async_copy(src, dst, load_sem.at[i])
        c.start()
        loads.append(c)
    g[CAP] = jnp.zeros(g.shape[1:], BF)
    p[CAP] = jnp.zeros(p.shape[1:], BF)
    for i in range(4):
        face[i, CAP] = jnp.zeros(face.shape[2:], BF)
    octs[24] = jnp.zeros(octs.shape[1:], BF)
    for s in range(8):
        part[3, s // 2, s % 2, 3, 2:4] = jnp.zeros((2, 16, 256), BF)
    loads[0].wait()
    loads[1].wait()
    pl.semaphore_wait(barrier, len(peers))

    def rcopy(src, dst, ss, rs, to):
        return pltpu.make_async_remote_copy(
            src_ref=src, dst_ref=dst, send_sem=ss, recv_sem=rs, device_id=to, device_id_type=MESH
        )

    halos = []
    for i, (src, to) in enumerate(
        (
            (p.at[0:CAP, 7], nxt),
            (p.at[0:CAP, 0], prv),
            (g.at[0:CAP, 7], nxt),
            (g.at[0:CAP, 0], prv),
        )
    ):
        c = rcopy(src, face.at[i, 0:CAP], halo_s.at[i], halo_r.at[i], to)
        c.start()
        halos.append(c)

    zi = lax.broadcasted_iota(jnp.int32, (10, 8, 256), 1)

    def expand(load, a, blk, plane, dst, relu):
        def slot(b, c):
            n = links[blk, 9 * (a + 1) + 3 * (b + 1) + (c + 1)]
            return jnp.where(n < 0, CAP, n)

        cols = []
        for c in (-1, 0, 1):
            low = load(slot(-1, c), pl.ds(48, 16)).astype(F32)[8:16]
            mid = load(slot(0, c), pl.ds(0, 64)).astype(F32)
            high = load(slot(1, c), pl.ds(0, 16)).astype(F32)[0:8]
            col = jnp.concatenate([low, mid, high], axis=0)
            if relu:
                col = jnp.maximum(col, 0.0)
            cols.append(col.reshape(10, 8, 256))
        shifted = (
            pltpu.roll(jnp.where(zi == 7, cols[0], cols[1]), 1, 1),
            cols[1],
            pltpu.roll(jnp.where(zi == 0, cols[2], cols[1]), 7, 1),
        )
        rows = pl.ds(pl.multiple_of(blk * 64, 64), 64)
        for ty in range(3):
            for tz in range(3):
                dst[3 * ty + tz, plane, rows] = shifted[tz][ty : ty + 8].reshape(64, 256).astype(BF)

    def inner(n, _):
        blk, x = n // 8, n % 8
        expand(lambda s, r: p[s, x, r], 0, blk, x + 1, ash, True)
        expand(lambda s, r: g[s, x, r], 0, blk, x + 1, gsh, False)
        return 0

    lax.fori_loop(0, CAP * 8, inner, 0)

    def transpose_plane(x, _):
        cols = pl.ds(pl.multiple_of(x * 2, 2), 2)
        gt[:, pl.ds(pl.multiple_of(x * 384, 384), 384)] = (
            gsh[4, pl.ds(1 + 2 * x, 2)].reshape(384, 256).T
        )
        return 0

    lax.fori_loop(0, 4, transpose_plane, 0)

    def tap(t, _):
        tx, tyz = t // 9, t % 9
        rows = ash[tyz, pl.ds(tx, 8)].reshape(1536, 256)
        grad = dot_nn(gt[...], rows).T.astype(BF)
        for i in range(8):
            m = t * 8 + i
            k, r = m // 27, m % 27
            q8 = r % 8
            part[r // 8, k // 2, k % 2, q8 // 2, pl.ds((q8 % 2) * 2, 2)] = grad[
                32 * i : 32 * i + 32
            ].reshape(2, 16, 256)
        return 0

    lax.fori_loop(9, 18, tap, 0)

    for c in halos:
        c.wait_recv()

    def outer(blk, _):
        expand(lambda s, r: face[0, s, r], -1, blk, 0, ash, True)
        expand(lambda s, r: face[1, s, r], 1, blk, 9, ash, True)
        expand(lambda s, r: face[2, s, r], -1, blk, 0, gsh, False)
        expand(lambda s, r: face[3, s, r], 1, blk, 9, gsh, False)
        return 0

    lax.fori_loop(0, CAP, outer, 0)
    lax.fori_loop(0, 9, tap, 0)
    lax.fori_loop(18, 27, tap, 0)

    flights = []

    def launch(grp, base, axis, src_of, dst_of):
        copies = []
        for off in (1, 2, 3):
            to = ring(axis, off)
            i = base + off - 1
            c = rcopy(
                src_of(to), dst_of(off - 1), red_s.at[grp, i], red_r.at[grp, i], dev(axis, to)
            )
            c.start()
            copies.append(c)
        flights.extend(copies)
        return copies

    def cut(ref, dims, axis, at):
        return ref.at[tuple(at if d == axis else slice(None) for d in dims)]

    class Group:
        def __init__(self, grp):
            self.grp = grp
            self.order = ORDERS[grp]
            self.done = 0

        def start(self):
            grp = self.grp
            self.copies = [
                rcopy(
                    part.at[grp, :, 1 - cc], rcore.at[grp], red_s.at[grp, 0], red_r.at[grp, 0],
                    partner,
                )
            ]
            self.copies[0].start()
            flights.extend(self.copies)

        def step(self):
            grp, order, n = self.grp, self.order, self.done
            self.done += 1
            for c in self.copies:
                c.wait_recv()
            if n == 0:
                for z in range(4):
                    racc[grp, z] = (
                        part[grp, z, cc].astype(F32) + rcore[grp, z].astype(F32)
                    ).astype(BF)
                src = racc.at[grp]
                dims = "zxy"
                self.copies = launch(
                    grp, 1, order[0], lambda to: cut(src, dims, order[0], to),
                    lambda s: r1.at[grp, s],
                )
                return
            if n == 1:
                mine = cut(racc.at[grp], "zxy", order[0], coord[order[0]])
                total = mine[...].astype(F32)
                for s in range(3):
                    total = total + r1[grp, s].astype(F32)
                a1[grp] = total.astype(BF)
                src = a1.at[grp]
                dims = "zxy".replace(order[0], "")
                self.copies = launch(
                    grp, 4, order[1], lambda to: cut(src, dims, order[1], to),
                    lambda s: r2.at[grp, s],
                )
                return
            if n == 2:
                dims = "zxy".replace(order[0], "")
                mine = cut(a1.at[grp], dims, order[1], coord[order[1]])
                total = mine[...].astype(F32)
                for s in range(3):
                    total = total + r2[grp, s].astype(F32)
                a2[grp] = total.astype(BF)
                src = a2.at[grp]
                self.copies = launch(
                    grp, 7, order[2], lambda to: src.at[to], lambda s: r3.at[grp, s]
                )
                return
            first, second = ("y", "x") if grp % 2 == 0 else ("x", "y")
            if n == 3:
                total = a2[grp, coord[order[2]]].astype(F32)
                for s in range(3):
                    total = total + r3[grp, s].astype(F32)
                red[grp, xc, yc] = total.astype(BF)
                spot = red.at[grp, xc, yc]
                self.copies = launch(grp, 10, first, lambda to: spot, lambda s: spot)
                return
            if n == 4:
                spot = cut(red.at[grp], "xy", second, coord[second])
                self.copies = launch(grp, 13, second, lambda to: spot, lambda s: spot)
                return

    groups = [Group(i) for i in range(GROUPS)]
    early, late = groups[:3], groups[3:]

    def step(some):
        for one in some:
            one.step()

    for one in early:
        one.start()
    loads[2].wait()

    def input_grad(half):
        def taps(tyz, _):
            lhs = jnp.concatenate(
                [gsh[8 - tyz, pl.ds(2 - i + 4 * half, 4)].reshape(768, 256) for i in range(3)],
                axis=1,
            )
            rhs = jnp.concatenate([w[9 * i + tyz] for i in range(3)], axis=1)
            res = dot_nt(lhs, rhs)
            acc[half] += res
            return 0

        acc[half] = jnp.zeros((768, 256), F32)
        lax.fori_loop(0, 9, taps, 0)

    lower = lax.broadcasted_iota(jnp.int32, (2, 8, 256), 1) < 4

    def octants(half):
        def plane(n, _):
            cx, blk = n // CAP, n % CAP
            val = acc[half, pl.ds(pl.multiple_of(n * 64, 64), 64)]
            pre = p[blk, 4 * half + cx].astype(F32)
            val = jnp.where(pre > 0.0, val, 0.0).reshape(2, 2, 2, 8, 256)
            for oy in range(2):
                even, odd = val[oy, :, 0], val[oy, :, 1]
                first = jnp.where(lower, even, pltpu.roll(odd, 4, 1))
                second = jnp.where(lower, pltpu.roll(even, 4, 1), odd)
                rows = pl.ds(pl.multiple_of(cx * 16, 16), 16)
                slot = blk * 8 + 4 * half + 2 * oy
                octs[slot, rows] = first.reshape(16, 256).astype(BF)
                octs[slot + 1, rows] = second.reshape(16, 256).astype(BF)
            return 0

        lax.fori_loop(0, 4 * CAP, plane, 0)

    input_grad(0)
    step(early)
    octants(0)
    input_grad(1)
    step(early)
    octants(1)

    def route(k):
        def place(j, _):
            e = routes[k, j]
            val = octs[jnp.where(e < 0, 24, e)]
            if k == 1:
                octin[8 + j] = val
            else:
                out[k // 2, j] = val
            return 0

        lax.fori_loop(0, 8, place, 0)

    route(0)
    passing = [rcopy(out.at[0], octin.at[0:8], oct_s.at[0], oct_r.at[0], prv)]
    passing[0].start()
    route(2)
    passing.append(rcopy(out.at[1], octin.at[16:24], oct_s.at[1], oct_r.at[1], nxt))
    passing[1].start()
    step(early)
    route(1)
    loads[3].wait()
    loads[4].wait()
    step(early)
    for c in passing:
        c.wait_recv()

    def turn(i, _):
        ot[:, pl.ds(pl.multiple_of(i * 384, 384), 384)] = (
            octin[pl.ds(6 * i, 6)].reshape(384, 256).T
        )
        return 0

    lax.fori_loop(0, 4, turn, 0)

    def down(i, _):
        rows = jnp.concatenate(
            [fine[:, 2 * i].reshape(1536, 128), fine[:, 2 * i + 1].reshape(1536, 128)], axis=1
        )
        grad = dot_nn(ot[...], rows).T.astype(BF)
        for c in range(2):
            one = grad[128 * c : 128 * c + 128]
            part[3, i, c, 1, 2:4] = one[0:32].reshape(2, 16, 256)
            part[3, i, c, 2] = one[32:96].reshape(4, 16, 256)
            part[3, i, c, 3, 0:2] = one[96:128].reshape(2, 16, 256)
        return 0

    lax.fori_loop(0, 4, down, 0)
    late[0].start()
    step(early)

    def fine_grad(i, _):
        at = pl.ds(4 * i, 4)
        res = dot_nt(octin[at].reshape(256, 256), dw[...]).astype(BF)
        for q in range(8):
            fg[at, q] = res[:, 128 * q : 128 * q + 128].reshape(4, 64, 128)
        return 0

    puts = []
    for i in range(3):
        lax.fori_loop(2 * i, 2 * i + 2, fine_grad, 0)
        c = pltpu.make_async_copy(
            fg.at[8 * i : 8 * i + 8], fg_hbm.at[8 * i : 8 * i + 8], fg_sem.at[i]
        )
        c.start()
        puts.append(c)
        step(late)
    step(late)
    step(late)
    for one in groups:
        for c in one.copies:
            c.wait_recv()
    c = pltpu.make_async_copy(red, red_hbm, fg_sem.at[3])
    c.start()
    puts.append(c)
    for c in halos + passing + flights:
        c.wait_send()
    for c in puts:
        c.wait()


def body(grad_out, pre_act, conv_weight, down_weight, fine_act, neighbours, octant_routes):
    slots, voxels, channels = grad_out.shape[1:]
    any_space = pl.BlockSpec(memory_space=pl.ANY)
    smem = pl.BlockSpec(memory_space=pltpu.SMEM)
    V = pltpu.VMEM
    fg, red = pl.pallas_call(
        kernel,
        out_shape=(
            jax.ShapeDtypeStruct((24, 8, 64, 128), BF),
            jax.ShapeDtypeStruct((GROUPS, 4, 4, 16, 256), BF),
        ),
        in_specs=[smem, smem] + [any_space] * 5,
        out_specs=(any_space, any_space),
        scratch_shapes=[
            V((CAP + 1, 8, 64, 256), BF),
            V((CAP + 1, 8, 64, 256), BF),
            V((4, CAP + 1, 64, 256), BF),
            V((9, 10, 192, 256), BF),
            V((9, 10, 192, 256), BF),
            V((256, 1536), BF),
            V((27, 256, 256), BF),
            V((1024, 256), BF),
            V((24, 8, 64, 128), BF),
            V((24, 8, 64, 128), BF),
            V((2, 768, 256), F32),
            V((25, 64, 256), BF),
            V((2, 8, 64, 256), BF),
            V((24, 64, 256), BF),
            V((256, 1536), BF),
            V((GROUPS, 4, 2, 4, 4, 16, 256), BF),
            V((GROUPS, 4, 4, 4, 16, 256), BF),
            V((GROUPS, 4, 4, 4, 16, 256), BF),
            V((GROUPS, 3, 4, 4, 16, 256), BF),
            V((GROUPS, 4, 4, 16, 256), BF),
            V((GROUPS, 3, 4, 16, 256), BF),
            V((GROUPS, 4, 16, 256), BF),
            V((GROUPS, 3, 16, 256), BF),
            V((GROUPS, 4, 4, 16, 256), BF),
            pltpu.SemaphoreType.DMA((5,)),
            pltpu.SemaphoreType.DMA((4,)),
            pltpu.SemaphoreType.DMA((4,)),
            pltpu.SemaphoreType.DMA((2,)),
            pltpu.SemaphoreType.DMA((2,)),
            pltpu.SemaphoreType.DMA((GROUPS, 16)),
            pltpu.SemaphoreType.DMA((GROUPS, 16)),
            pltpu.SemaphoreType.DMA((4,)),
        ],
        compiler_params=pltpu.CompilerParams(
            collective_id=0, has_side_effects=True, vmem_limit_bytes=60 * 1024 * 1024
        ),
        name="backward",
    )(
        neighbours[0],
        octant_routes[0, 0],
        grad_out[0].reshape(slots, 8, 64, channels),
        pre_act[0].reshape(slots, 8, 64, channels),
        conv_weight,
        down_weight.reshape(1024, 256),
        fine_act[0].reshape(24, 8, 64, 128),
    )
    factor = 1.0 / math.sqrt(lax.axis_size("dp") * lax.axis_size("dom") * slots * voxels)
    total = red.reshape(1024, 256).astype(F32) * factor
    return (fg.reshape(fine_act.shape), total[:864], total[864:992])


def solution(mesh):
    return jax.shard_map(
        body,
        mesh=mesh,
        in_specs=(
            P("dp", "dom", None, None),
            P("dp", "dom", None, None),
            P(),
            P(),
            P("dp", "dom", None, None),
            P("dp", "dom", None),
            P("dp", "dom", None, None),
        ),
        out_specs=(P("dp", "dom", None, None), P("dp", None), P("dp", None)),
        check_vma=False,
    )
```

```python
import math

import jax
import jax.numpy as jnp
from jax import lax
from jax.experimental import pallas as pl
from jax.experimental.pallas import tpu as pltpu
from jax.sharding import PartitionSpec as P

MESH = pl.DeviceIdType.MESH
BF = jnp.bfloat16
F32 = jnp.float32
CAP = 3
GROUPS = 4
FIRST = "xyzz"


def dot_nt(a, b):
    return lax.dot_general(a, b, (((1,), (1,)), ((), ())), preferred_element_type=F32)


def dot_nn(a, b):
    return lax.dot_general(a, b, (((1,), (0,)), ((), ())), preferred_element_type=F32)


def kernel(
    links, routes, g_hbm, p_hbm, w_hbm, dw_hbm, fine_hbm,
    fg_hbm, conv_hbm, down_hbm,
    g, p, face, pface, gsh, ash, gt, w, dw, fine, fg, acc, octs, out, octin, ot,
    part, rcore, racc, r1, s1, a1, r2, red, conv,
    load_sem, halo_s, halo_r, oct_s, oct_r, red_s, red_r, fg_sem,
):
    dp = lax.axis_index("dp")
    dom = lax.axis_index("dom")
    zc, cc = dp // 2, dp % 2
    yc, xc = dom // 4, dom % 4
    coord = {"z": zc, "x": xc, "y": yc}

    def at_offset(**offsets):
        z, x, y = (lax.rem(coord[a] + offsets.get(a, 0), 4) for a in "zxy")
        return (z * 2 + cc, y * 4 + x)

    partner = (zc * 2 + (1 - cc), dom)
    nxt = (dp, lax.rem(dom + 1, 16))
    prv = (dp, lax.rem(dom + 15, 16))

    barrier = pltpu.get_barrier_semaphore()
    peers = [partner, nxt, prv]
    for z in range(4):
        for x in range(4):
            for y in range(4):
                if (z, x, y) != (0, 0, 0) and 0 in (z, x, y):
                    peers.append(at_offset(z=z, x=x, y=y))
    for peer in peers:
        pl.semaphore_signal(barrier, inc=1, device_id=peer, device_id_type=MESH)

    loads = []
    for i, (src, dst) in enumerate(
        ((g_hbm, g.at[0:CAP]), (p_hbm, p.at[0:CAP]), (w_hbm, w), (fine_hbm, fine), (dw_hbm, dw))
    ):
        c = pltpu.make_async_copy(src, dst, load_sem.at[i])
        c.start()
        loads.append(c)
    g[CAP] = jnp.zeros(g.shape[1:], BF)
    p[CAP] = jnp.zeros(p.shape[1:], BF)
    for i in range(2):
        face[i, CAP] = jnp.zeros(face.shape[2:], BF)
        pface[i, CAP] = jnp.zeros(face.shape[2:], BF)
    octs[24] = jnp.zeros(octs.shape[1:], BF)
    for s in range(8):
        part[3, s // 2, s % 2, 3, 2:4] = jnp.zeros((2, 16, 256), BF)
    loads[0].wait()
    loads[1].wait()
    pl.semaphore_wait(barrier, len(peers))

    def rcopy(src, dst, ss, rs, to):
        return pltpu.make_async_remote_copy(
            src_ref=src, dst_ref=dst, send_sem=ss, recv_sem=rs, device_id=to, device_id_type=MESH
        )

    halos = []
    for i, (src, dst, to) in enumerate(
        (
            (g.at[0:CAP, 7], face.at[0], nxt),
            (g.at[0:CAP, 0], face.at[1], prv),
            (p.at[0:CAP, 7], pface.at[0], nxt),
            (p.at[0:CAP, 0], pface.at[1], prv),
        )
    ):
        c = rcopy(src, dst.at[0:CAP], halo_s.at[i], halo_r.at[i], to)
        c.start()
        halos.append(c)

    zi = lax.broadcasted_iota(jnp.int32, (10, 8, 256), 1)

    def expand(load, a, blk, plane, dst, relu):
        def slot(b, c):
            n = links[blk, 0, 9 * (a + 1) + 3 * (b + 1) + (c + 1)]
            return jnp.where(n < 0, CAP, n)

        cols = []
        for c in (-1, 0, 1):
            low = load(slot(-1, c), pl.ds(48, 16)).astype(F32)[8:16]
            mid = load(slot(0, c), pl.ds(0, 64)).astype(F32)
            high = load(slot(1, c), pl.ds(0, 16)).astype(F32)[0:8]
            col = jnp.concatenate([low, mid, high], axis=0)
            if relu:
                col = jnp.maximum(col, 0.0)
            cols.append(col.reshape(10, 8, 256))
        shifted = (
            pltpu.roll(jnp.where(zi == 7, cols[0], cols[1]), 1, 1),
            cols[1],
            pltpu.roll(jnp.where(zi == 0, cols[2], cols[1]), 7, 1),
        )
        rows = pl.ds(pl.multiple_of(blk * 64, 64), 64)
        for ty in range(3):
            for tz in range(3):
                dst[3 * ty + tz, plane, rows] = shifted[tz][ty : ty + 8].reshape(64, 256).astype(BF)

    def inner_g(n, _):
        blk, x = n // 8, n % 8
        expand(lambda s, r: g[s, x, r], 0, blk, x + 1, gsh, False)
        return 0

    def outer_g(blk, _):
        expand(lambda s, r: face[0, s, r], -1, blk, 0, gsh, False)
        expand(lambda s, r: face[1, s, r], 1, blk, 9, gsh, False)
        return 0

    def inner_p(n, _):
        blk, x = n // 8, n % 8
        expand(lambda s, r: p[s, x, r], 0, blk, x + 1, ash, True)
        return 0

    def outer_p(blk, _):
        expand(lambda s, r: pface[0, s, r], -1, blk, 0, ash, True)
        expand(lambda s, r: pface[1, s, r], 1, blk, 9, ash, True)
        return 0

    def input_grad(half, first, last):
        def taps(n, _):
            tx, ty = n // 3, n % 3
            lhs = jnp.concatenate(
                [
                    gsh[8 - 3 * ty - tz, pl.ds(2 - tx + 4 * half, 4)].reshape(768, 256)
                    for tz in range(3)
                ],
                axis=1,
            )
            rhs = jnp.concatenate([w[3 * n + tz] for tz in range(3)], axis=1)
            acc[half] += dot_nt(lhs, rhs)
            return 0

        lax.fori_loop(first, last, taps, 0)

    lower = lax.broadcasted_iota(jnp.int32, (2, 8, 256), 1) < 4

    def octants(half):
        def plane(n, _):
            cx, blk = n // CAP, n % CAP
            val = acc[half, pl.ds(pl.multiple_of(n * 64, 64), 64)]
            pre = p[blk, 4 * half + cx].astype(F32)
            val = jnp.where(pre > 0.0, val, 0.0).reshape(2, 2, 2, 8, 256)
            for oy in range(2):
                even, odd = val[oy, :, 0], val[oy, :, 1]
                first = jnp.where(lower, even, pltpu.roll(odd, 4, 1))
                second = jnp.where(lower, pltpu.roll(even, 4, 1), odd)
                rows = pl.ds(pl.multiple_of(cx * 16, 16), 16)
                slot = blk * 8 + 4 * half + 2 * oy
                octs[slot, rows] = first.reshape(16, 256).astype(BF)
                octs[slot + 1, rows] = second.reshape(16, 256).astype(BF)
            return 0

        lax.fori_loop(0, 4 * CAP, plane, 0)

    passing = []

    def route(half):
        def place(k):
            def one(j, _):
                e = routes[0, k, 0, j]
                val = octs[jnp.where(e < 0, 24, e)]
                if k == 1:
                    octin[8 + j] = val
                else:
                    out[k // 2, j] = val
                return 0

            lax.fori_loop(4 * half, 4 * half + 4, one, 0)

        place(0)
        place(2)
        for k, base, to in ((0, 0, prv), (1, 16, nxt)):
            i = 2 * half + k
            c = rcopy(
                out.at[k, 4 * half : 4 * half + 4],
                octin.at[base + 4 * half : base + 4 * half + 4],
                oct_s.at[i], oct_r.at[i], to,
            )
            c.start()
            passing.append(c)
        place(1)

    acc[...] = jnp.zeros(acc.shape, F32)
    lax.fori_loop(0, CAP * 8, inner_g, 0)
    loads[2].wait()
    input_grad(0, 3, 6)
    input_grad(1, 3, 6)
    halos[0].wait_recv()
    halos[1].wait_recv()
    lax.fori_loop(0, CAP, outer_g, 0)
    for half in range(2):
        input_grad(half, 0, 3)
        input_grad(half, 6, 9)
        octants(half)
        route(half)

    lax.fori_loop(0, CAP * 8, inner_p, 0)
    halos[2].wait_recv()
    halos[3].wait_recv()
    lax.fori_loop(0, CAP, outer_p, 0)

    def transpose_plane(x, _):
        gt[:, pl.ds(pl.multiple_of(x * 384, 384), 384)] = (
            gsh[4, pl.ds(1 + 2 * x, 2)].reshape(384, 256).T
        )
        return 0

    lax.fori_loop(0, 4, transpose_plane, 0)

    def tap(t):
        tx, tyz = t // 9, t % 9
        rows = ash[tyz, pl.ds(tx, 8)].reshape(1536, 256)
        return dot_nn(gt[...], rows).T.astype(BF)

    def whole_tap(shift):
        def one(k, _):
            part[shift, k // 2, k % 2] = tap((27 * k + 7) // 8 + shift).reshape(4, 4, 16, 256)
            return 0

        return one

    def split_tap(n, _):
        t = 2 + n
        for at, jump in ((2, 2), (3, 2), (5, 2), (6, 2), (7, 2), (9, 2), (10, 2)):
            t = t + jnp.where(n >= at, jump, 0)
        grad = tap(t)
        for i in range(8):
            m = t * 8 + i
            k, r = m // 27, m % 27
            pos = jnp.where(t < (27 * k + 7) // 8, r, r - 16)
            q8 = pos % 8
            part[2 + pos // 8, k // 2, k % 2, q8 // 2, pl.ds((q8 % 2) * 2, 2)] = grad[
                32 * i : 32 * i + 32
            ].reshape(2, 16, 256)
        return 0

    def cut(ref, axis, at):
        return ref.at[tuple(at if d == axis else slice(None) for d in "zxy")]

    class Group:
        def __init__(self, grp):
            self.grp = grp
            self.axis = FIRST[grp]
            self.stage = 0
            self.sends = []

        def send(self, src, dst, i, to):
            c = rcopy(src, dst, red_s.at[self.grp, i], red_r.at[self.grp, i], to)
            c.start()
            if i < 7:
                self.sends.append(c)
            return c

        def all_of(self, i):
            return rcopy(
                r2.at[self.grp], r2.at[self.grp], red_s.at[self.grp, i], red_r.at[self.grp, i],
                partner,
            )

        def chunk(self, off, half):
            ref = cut(racc.at[self.grp], self.axis, lax.rem(coord[self.axis] + off, 4))
            return ref.at[2 * half : 2 * half + 2]

        def step(self):
            grp, axis = self.grp, self.axis
            left, right = at_offset(**{axis: 3}), at_offset(**{axis: 1})
            stage = self.stage
            self.stage += 1
            if stage == 0:
                self.core = self.send(part.at[grp, :, 1 - cc], rcore.at[grp], 0, partner)
            elif stage == 1:
                self.core.wait_recv()
                for z in range(4):
                    racc[grp, z] = (
                        part[grp, z, cc].astype(F32) + rcore[grp, z].astype(F32)
                    ).astype(BF)
                box = r1.at[grp]
                self.relay_a = self.send(self.chunk(2, 0), box.at[0], 1, right)
                self.relay_b = self.send(self.chunk(2, 1), box.at[1], 2, left)
                self.direct_b = self.send(self.chunk(1, 1), box.at[2], 3, right)
                self.direct_a = self.send(self.chunk(3, 0), box.at[3], 4, left)
            elif stage == 2:
                box = r1.at[grp]
                self.relay_a.wait_recv()
                s1[grp, 0] = (self.chunk(1, 0)[...].astype(F32) + r1[grp, 0].astype(F32)).astype(BF)
                self.sum_a = self.send(s1.at[grp, 0], box.at[4], 5, right)
                self.relay_b.wait_recv()
                s1[grp, 1] = (self.chunk(3, 1)[...].astype(F32) + r1[grp, 1].astype(F32)).astype(BF)
                self.sum_b = self.send(s1.at[grp, 1], box.at[5], 6, left)
            elif stage == 3:
                for c in (self.direct_a, self.direct_b, self.sum_a, self.sum_b):
                    c.wait_recv()
                for half, (i, j) in enumerate(((4, 3), (5, 2))):
                    total = self.chunk(0, half)[...].astype(F32)
                    total = total + r1[grp, i].astype(F32) + r1[grp, j].astype(F32)
                    a1[grp, 2 * half : 2 * half + 2] = total.astype(BF)
                u, v = "zxy".replace(axis, "")
                for n in range(1, 16):
                    du, dv = n // 4, n % 4
                    src = a1.at[grp, lax.rem(coord[u] + du, 4), lax.rem(coord[v] + dv, 4)]
                    self.send(src, r2.at[grp, n - 1], 7, at_offset(**{u: du, v: dv}))
            elif stage == 4:
                self.all_of(7).wait_recv()
                u, v = "zxy".replace(axis, "")
                total = a1[grp, coord[u], coord[v]].astype(F32)
                for n in range(15):
                    total = total + r2[grp, n].astype(F32)
                red[grp, xc, yc] = total.astype(BF)
                spot = red.at[grp, xc, yc]
                for n in range(1, 16):
                    self.send(spot, spot, 8, at_offset(x=n // 4, y=n % 4))
            else:
                self.all_of(8).wait_recv()

        def finish(self):
            for c in self.sends:
                c.wait_send()
            self.all_of(7).wait_send()
            self.all_of(8).wait_send()

    ga, gb, gc, gd = (Group(i) for i in range(GROUPS))

    lax.fori_loop(0, 11, split_tap, 0)
    gc.step()
    lax.fori_loop(0, 8, whole_tap(0), 0)
    ga.step()
    gc.step()
    lax.fori_loop(0, 4, whole_tap(1), 0)
    gc.step()
    ga.step()
    lax.fori_loop(4, 8, whole_tap(1), 0)
    gb.step()

    for c in passing:
        c.wait_recv()
    loads[3].wait()
    loads[4].wait()

    def turn(i, _):
        ot[:, pl.ds(pl.multiple_of(i * 384, 384), 384)] = (
            octin[pl.ds(6 * i, 6)].reshape(384, 256).T
        )
        return 0

    lax.fori_loop(0, 4, turn, 0)

    def down(i, _):
        rows = jnp.concatenate(
            [fine[:, 2 * i].reshape(1536, 128), fine[:, 2 * i + 1].reshape(1536, 128)], axis=1
        )
        grad = dot_nn(ot[...], rows).T.astype(BF)
        for c in range(2):
            one = grad[128 * c : 128 * c + 128]
            part[3, i, c, 1, 2:4] = one[0:32].reshape(2, 16, 256)
            part[3, i, c, 2] = one[32:96].reshape(4, 16, 256)
            part[3, i, c, 3, 0:2] = one[96:128].reshape(2, 16, 256)
        return 0

    lax.fori_loop(0, 4, down, 0)
    gd.step()
    gc.step()
    ga.step()

    def fine_grad(i, _):
        at = pl.ds(4 * i, 4)
        res = dot_nt(octin[at].reshape(256, 256), dw[...]).astype(BF)
        for q in range(8):
            fg[at, q] = res[:, 128 * q : 128 * q + 128].reshape(4, 64, 128)
        return 0

    puts = []

    def fine_part(i):
        lax.fori_loop(2 * i, 2 * i + 2, fine_grad, 0)
        c = pltpu.make_async_copy(
            fg.at[8 * i : 8 * i + 8], fg_hbm.at[8 * i : 8 * i + 8], fg_sem.at[i]
        )
        c.start()
        puts.append(c)

    fine_part(0)
    gb.step()
    fine_part(1)
    gd.step()
    fine_part(2)
    for one in (ga, gc, gb, gd, gb, ga, gd, gc, gb, ga, gd, gb, gd):
        one.step()

    k = dp
    lead = (27 * k + 7) // 8 * 8 - 27 * k
    start = pl.multiple_of(lead * 32, 32)
    conv[pl.ds(start, 256)] = red[0].reshape(256, 256)
    conv[pl.ds(start + 256, 256)] = red[1].reshape(256, 256)
    for n in range(11):
        row = 32 * (n + jnp.where(n < lead, 0, 16))
        piece = red[2 + n // 8, n % 8 // 2, (n % 2) * 2 : (n % 2) * 2 + 2]
        conv[pl.ds(pl.multiple_of(row, 32), 32)] = piece.reshape(32, 256)
    conv[864:896] = red[3, 1, 2:4].reshape(32, 256)
    conv[896:960] = red[3, 2].reshape(64, 256)
    conv[960:992] = red[3, 3, 0:2].reshape(32, 256)
    for i, (src, dst) in enumerate(((conv.at[0:864], conv_hbm), (conv.at[864:992], down_hbm))):
        c = pltpu.make_async_copy(src, dst, fg_sem.at[3 + i])
        c.start()
        puts.append(c)
    for c in halos + passing:
        c.wait_send()
    for one in (ga, gb, gc, gd):
        one.finish()
    for c in puts:
        c.wait()


def body(grad_out, pre_act, conv_weight, down_weight, fine_act, neighbours, octant_routes):
    slots, voxels, channels = grad_out.shape[1:]
    any_space = pl.BlockSpec(memory_space=pl.ANY)
    smem = pl.BlockSpec(memory_space=pltpu.SMEM)
    V = pltpu.VMEM
    fg, conv, down = pl.pallas_call(
        kernel,
        out_shape=(
            jax.ShapeDtypeStruct((24, 8, 64, 128), BF),
            jax.ShapeDtypeStruct((864, 256), BF),
            jax.ShapeDtypeStruct((128, 256), BF),
        ),
        in_specs=[smem, smem] + [any_space] * 5,
        out_specs=(any_space, any_space, any_space),
        scratch_shapes=[
            V((CAP + 1, 8, 64, 256), BF),
            V((CAP + 1, 8, 64, 256), BF),
            V((2, CAP + 1, 64, 256), BF),
            V((2, CAP + 1, 64, 256), BF),
            V((9, 10, 192, 256), BF),
            V((9, 10, 192, 256), BF),
            V((256, 1536), BF),
            V((27, 256, 256), BF),
            V((1024, 256), BF),
            V((24, 8, 64, 128), BF),
            V((24, 8, 64, 128), BF),
            V((2, 768, 256), F32),
            V((25, 64, 256), BF),
            V((2, 8, 64, 256), BF),
            V((24, 64, 256), BF),
            V((256, 1536), BF),
            V((GROUPS, 4, 2, 4, 4, 16, 256), BF),
            V((GROUPS, 4, 4, 4, 16, 256), BF),
            V((GROUPS, 4, 4, 4, 16, 256), BF),
            V((GROUPS, 6, 2, 4, 16, 256), BF),
            V((GROUPS, 2, 2, 4, 16, 256), BF),
            V((GROUPS, 4, 4, 16, 256), BF),
            V((GROUPS, 15, 16, 256), BF),
            V((GROUPS, 4, 4, 16, 256), BF),
            V((992, 256), BF),
            pltpu.SemaphoreType.DMA((5,)),
            pltpu.SemaphoreType.DMA((4,)),
            pltpu.SemaphoreType.DMA((4,)),
            pltpu.SemaphoreType.DMA((4,)),
            pltpu.SemaphoreType.DMA((4,)),
            pltpu.SemaphoreType.DMA((GROUPS, 9)),
            pltpu.SemaphoreType.DMA((GROUPS, 9)),
            pltpu.SemaphoreType.DMA((5,)),
        ],
        compiler_params=pltpu.CompilerParams(
            collective_id=0, has_side_effects=True, vmem_limit_bytes=60 * 1024 * 1024
        ),
        name="backward",
    )(
        neighbours.transpose(1, 0, 2),
        octant_routes.transpose(0, 2, 1, 3),
        grad_out[0].reshape(slots, 8, 64, channels),
        pre_act[0].reshape(slots, 8, 64, channels),
        conv_weight,
        down_weight.reshape(1024, 256),
        fine_act[0].reshape(24, 8, 64, 128),
    )
    factor = 1.0 / math.sqrt(lax.axis_size("dp") * lax.axis_size("dom") * slots * voxels)
    return (fg.reshape(fine_act.shape), conv.astype(F32) * factor, down.astype(F32) * factor)


def solution(mesh):
    return jax.shard_map(
        body,
        mesh=mesh,
        in_specs=(
            P("dp", "dom", None, None),
            P("dp", "dom", None, None),
            P(),
            P(),
            P("dp", "dom", None, None),
            P("dp", "dom", None),
            P("dp", "dom", None, None),
        ),
        out_specs=(P("dp", "dom", None, None), P("dp", None), P("dp", None)),
        check_vma=False,
    )
```

```python
import math

import jax
import jax.numpy as jnp
from jax import lax
from jax.experimental import pallas as pl
from jax.experimental.pallas import tpu as pltpu
from jax.sharding import PartitionSpec as P

MESH = pl.DeviceIdType.MESH
BF = jnp.bfloat16
F32 = jnp.float32
CAP = 3
GROUPS = 4
FLOWS = ((2, 0, 256, "z"), (3, 0, 128, "y"), (3, 128, 128, "x"), (0, 0, 256, "x"), (1, 0, 128, "z"), (1, 128, 128, "y"))


def dot_nt(a, b):
    return lax.dot_general(a, b, (((1,), (1,)), ((), ())), preferred_element_type=F32)


def dot_nn(a, b):
    return lax.dot_general(a, b, (((1,), (0,)), ((), ())), preferred_element_type=F32)


def kernel(
    links, routes, g_hbm, p_hbm, w_hbm, fine_hbm,
    octin_hbm, conv_hbm, down_hbm,
    g, p, face, pface, gsh, ash, gt, w, fine, acc, octs, out, octin, ot,
    part, rcore, racc, r1, s1, a1, r2, red, conv,
    load_sem, halo_s, halo_r, oct_s, oct_r, red_s, red_r, put_sem,
):
    dp = lax.axis_index("dp")
    dom = lax.axis_index("dom")
    zc, cc = dp // 2, dp % 2
    yc, xc = dom // 4, dom % 4
    coord = {"z": zc, "x": xc, "y": yc}

    def at_offset(**offsets):
        z, x, y = (lax.rem(coord[a] + offsets.get(a, 0), 4) for a in "zxy")
        return (z * 2 + cc, y * 4 + x)

    partner = (zc * 2 + (1 - cc), dom)
    nxt = (dp, lax.rem(dom + 1, 16))
    prv = (dp, lax.rem(dom + 15, 16))

    barrier = pltpu.get_barrier_semaphore()
    peers = [partner, nxt, prv]
    for z in range(4):
        for x in range(4):
            for y in range(4):
                if (z, x, y) != (0, 0, 0) and 0 in (z, x, y):
                    peers.append(at_offset(z=z, x=x, y=y))
    for peer in peers:
        pl.semaphore_signal(barrier, inc=1, device_id=peer, device_id_type=MESH)

    loads = []
    for i, (src, dst) in enumerate(
        ((g_hbm, g.at[0:CAP]), (p_hbm, p.at[0:CAP]), (w_hbm, w), (fine_hbm, fine))
    ):
        c = pltpu.make_async_copy(src, dst, load_sem.at[i])
        c.start()
        loads.append(c)
    g[CAP] = jnp.zeros(g.shape[1:], BF)
    p[CAP] = jnp.zeros(p.shape[1:], BF)
    for i in range(2):
        face[i, CAP] = jnp.zeros(face.shape[2:], BF)
        pface[i, CAP] = jnp.zeros(face.shape[2:], BF)
    octs[24] = jnp.zeros(octs.shape[1:], BF)
    for s in range(8):
        part[3, s // 2, s % 2, 3, 2:4] = jnp.zeros((2, 16, 256), BF)
    loads[0].wait()
    loads[1].wait()

    def rcopy(src, dst, ss, rs, to):
        return pltpu.make_async_remote_copy(
            src_ref=src, dst_ref=dst, send_sem=ss, recv_sem=rs, device_id=to, device_id_type=MESH
        )

    zi = lax.broadcasted_iota(jnp.int32, (10, 8, 256), 1)

    def expand(load, a, blk, plane, dst, relu):
        def slot(b, c):
            n = links[blk, 0, 9 * (a + 1) + 3 * (b + 1) + (c + 1)]
            return jnp.where(n < 0, CAP, n)

        cols = []
        for c in (-1, 0, 1):
            low = load(slot(-1, c), pl.ds(48, 16)).astype(F32)[8:16]
            mid = load(slot(0, c), pl.ds(0, 64)).astype(F32)
            high = load(slot(1, c), pl.ds(0, 16)).astype(F32)[0:8]
            col = jnp.concatenate([low, mid, high], axis=0)
            if relu:
                col = jnp.maximum(col, 0.0)
            cols.append(col.reshape(10, 8, 256))
        shifted = (
            pltpu.roll(jnp.where(zi == 7, cols[0], cols[1]), 1, 1),
            cols[1],
            pltpu.roll(jnp.where(zi == 0, cols[2], cols[1]), 7, 1),
        )
        rows = pl.ds(pl.multiple_of(blk * 64, 64), 64)
        for ty in range(3):
            for tz in range(3):
                dst[3 * ty + tz, plane, rows] = shifted[tz][ty : ty + 8].reshape(64, 256).astype(BF)

    def inner_g(n, _):
        blk, x = n // 8, n % 8
        expand(lambda s, r: g[s, x, r], 0, blk, x + 1, gsh, False)
        return 0

    def outer_g(blk, _):
        expand(lambda s, r: face[0, s, r], -1, blk, 0, gsh, False)
        expand(lambda s, r: face[1, s, r], 1, blk, 9, gsh, False)
        return 0

    def inner_p(n, _):
        blk, x = n // 8, n % 8
        expand(lambda s, r: p[s, x, r], 0, blk, x + 1, ash, True)
        return 0

    def outer_p(blk, _):
        expand(lambda s, r: pface[0, s, r], -1, blk, 0, ash, True)
        expand(lambda s, r: pface[1, s, r], 1, blk, 9, ash, True)
        return 0

    def input_grad(half, first, last):
        def taps(n, _):
            tx, ty = n // 3, n % 3
            lhs = jnp.concatenate(
                [
                    gsh[8 - 3 * ty - tz, pl.ds(2 - tx + 4 * half, 4)].reshape(768, 256)
                    for tz in range(3)
                ],
                axis=1,
            )
            rhs = jnp.concatenate([w[3 * n + tz] for tz in range(3)], axis=1)
            acc[half] += dot_nt(lhs, rhs)
            return 0

        lax.fori_loop(first, last, taps, 0)

    lower = lax.broadcasted_iota(jnp.int32, (2, 8, 256), 1) < 4

    def octants(half):
        def plane(n, _):
            cx, blk = n // CAP, n % CAP
            val = acc[half, pl.ds(pl.multiple_of(n * 64, 64), 64)]
            pre = p[blk, 4 * half + cx].astype(F32)
            val = jnp.where(pre > 0.0, val, 0.0).reshape(2, 2, 2, 8, 256)
            for oy in range(2):
                even, odd = val[oy, :, 0], val[oy, :, 1]
                first = jnp.where(lower, even, pltpu.roll(odd, 4, 1))
                second = jnp.where(lower, pltpu.roll(even, 4, 1), odd)
                rows = pl.ds(pl.multiple_of(cx * 16, 16), 16)
                slot = blk * 8 + 4 * half + 2 * oy
                octs[slot, rows] = first.reshape(16, 256).astype(BF)
                octs[slot + 1, rows] = second.reshape(16, 256).astype(BF)
            return 0

        lax.fori_loop(0, 4 * CAP, plane, 0)

    passing = []

    def route(half):
        def place(k):
            def one(j, _):
                e = routes[0, k, 0, j]
                val = octs[jnp.where(e < 0, 24, e)]
                if k == 1:
                    octin[8 + j] = val
                else:
                    out[k // 2, j] = val
                return 0

            lax.fori_loop(4 * half, 4 * half + 4, one, 0)

        place(0)
        place(2)
        for k, base, to in ((0, 0, prv), (1, 16, nxt)):
            i = 2 * half + k
            c = rcopy(
                out.at[k, 4 * half : 4 * half + 4],
                octin.at[base + 4 * half : base + 4 * half + 4],
                oct_s.at[i], oct_r.at[i], to,
            )
            c.start()
            passing.append(c)
        place(1)

    acc[...] = jnp.zeros(acc.shape, F32)
    lax.fori_loop(0, CAP * 8, inner_g, 0)
    pl.semaphore_wait(barrier, len(peers))

    halos = []
    for i, (src, dst, to) in enumerate(
        (
            (g.at[0:CAP, 7], face.at[0], nxt),
            (g.at[0:CAP, 0], face.at[1], prv),
            (p.at[0:CAP, 7], pface.at[0], nxt),
            (p.at[0:CAP, 0], pface.at[1], prv),
        )
    ):
        c = rcopy(src, dst.at[0:CAP], halo_s.at[i], halo_r.at[i], to)
        c.start()
        halos.append(c)

    loads[2].wait()
    input_grad(0, 3, 6)
    input_grad(1, 3, 6)
    halos[0].wait_recv()
    halos[1].wait_recv()
    lax.fori_loop(0, CAP, outer_g, 0)
    for half in range(2):
        input_grad(half, 0, 3)
        input_grad(half, 6, 9)
        octants(half)
        route(half)

    lax.fori_loop(0, CAP * 8, inner_p, 0)
    halos[2].wait_recv()
    halos[3].wait_recv()
    lax.fori_loop(0, CAP, outer_p, 0)

    def transpose_plane(x, _):
        gt[:, pl.ds(pl.multiple_of(x * 384, 384), 384)] = (
            gsh[4, pl.ds(1 + 2 * x, 2)].reshape(384, 256).T
        )
        return 0

    lax.fori_loop(0, 4, transpose_plane, 0)

    def tap(t):
        tx, tyz = t // 9, t % 9
        rows = ash[tyz, pl.ds(tx, 8)].reshape(1536, 256)
        return dot_nn(gt[...], rows).T.astype(BF)

    def whole_tap(shift):
        def one(k, _):
            part[shift, k // 2, k % 2] = tap((27 * k + 7) // 8 + shift).reshape(4, 4, 16, 256)
            return 0

        return one

    def split_tap(n, _):
        t = 2 + n
        for at, jump in ((2, 2), (3, 2), (5, 2), (6, 2), (7, 2), (9, 2), (10, 2)):
            t = t + jnp.where(n >= at, jump, 0)
        grad = tap(t)
        for i in range(8):
            m = t * 8 + i
            k, r = m // 27, m % 27
            pos = jnp.where(t < (27 * k + 7) // 8, r, r - 16)
            q8 = pos % 8
            part[2 + pos // 8, k // 2, k % 2, q8 // 2, pl.ds((q8 % 2) * 2, 2)] = grad[
                32 * i : 32 * i + 32
            ].reshape(2, 16, 256)
        return 0

    def cut(ref, axis, at):
        return ref.at[tuple(at if d == axis else slice(None) for d in "zxy")]

    class Flow:
        def __init__(self, n):
            self.n = n
            grp, lane, width, self.axis = FLOWS[n]
            lanes = pl.ds(lane, width)
            self.part = part.at[grp, :, :, :, :, :, lanes]
            self.rcore = rcore.at[grp, :, :, :, :, lanes]
            self.racc = racc.at[grp, :, :, :, :, lanes]
            self.r1 = r1.at[grp, :, :, :, :, lanes]
            self.s1 = s1.at[grp, :, :, :, :, lanes]
            self.a1 = a1.at[grp, :, :, :, lanes]
            self.r2 = r2.at[grp, :, :, lanes]
            self.red = red.at[grp, :, :, :, lanes]
            self.stage = 0
            self.sends = []

        def send(self, src, dst, i, to):
            c = rcopy(src, dst, red_s.at[self.n, i], red_r.at[self.n, i], to)
            c.start()
            if i < 7:
                self.sends.append(c)
            return c

        def all_of(self, i):
            return rcopy(self.r2, self.r2, red_s.at[self.n, i], red_r.at[self.n, i], partner)

        def chunk(self, off, half):
            ref = cut(self.racc, self.axis, lax.rem(coord[self.axis] + off, 4))
            return ref.at[2 * half : 2 * half + 2]

        def step(self):
            axis = self.axis
            left, right = at_offset(**{axis: 3}), at_offset(**{axis: 1})
            u, v = "zxy".replace(axis, "")
            stage = self.stage
            self.stage += 1
            if stage == 0:
                self.core = self.send(self.part.at[:, 1 - cc], self.rcore, 0, partner)
            elif stage == 1:
                self.core.wait_recv()
                for z in range(4):
                    self.racc[z] = (
                        self.part[z, cc].astype(F32) + self.rcore[z].astype(F32)
                    ).astype(BF)
                box = self.r1
                self.relay_a = self.send(self.chunk(2, 0), box.at[0], 1, right)
                self.relay_b = self.send(self.chunk(2, 1), box.at[1], 2, left)
                self.direct_b = self.send(self.chunk(1, 1), box.at[2], 3, right)
                self.direct_a = self.send(self.chunk(3, 0), box.at[3], 4, left)
            elif stage == 2:
                box = self.r1
                self.relay_a.wait_recv()
                self.s1[0] = (self.chunk(1, 0)[...].astype(F32) + box[0].astype(F32)).astype(BF)
                self.sum_a = self.send(self.s1.at[0], box.at[4], 5, right)
                self.relay_b.wait_recv()
                self.s1[1] = (self.chunk(3, 1)[...].astype(F32) + box[1].astype(F32)).astype(BF)
                self.sum_b = self.send(self.s1.at[1], box.at[5], 6, left)
            elif stage == 3:
                for c in (self.direct_a, self.direct_b, self.sum_a, self.sum_b):
                    c.wait_recv()
                for half, (i, j) in enumerate(((4, 3), (5, 2))):
                    total = self.chunk(0, half)[...].astype(F32)
                    total = total + self.r1[i].astype(F32) + self.r1[j].astype(F32)
                    self.a1[2 * half : 2 * half + 2] = total.astype(BF)
                for n in range(1, 16):
                    du, dv = n // 4, n % 4
                    src = self.a1.at[lax.rem(coord[u] + du, 4), lax.rem(coord[v] + dv, 4)]
                    self.send(src, self.r2.at[n - 1], 7, at_offset(**{u: du, v: dv}))
            elif stage == 4:
                self.all_of(7).wait_recv()
                total = self.a1[coord[u], coord[v]].astype(F32)
                for n in range(15):
                    total = total + self.r2[n].astype(F32)
                self.red[xc, yc] = total.astype(BF)
                spot = self.red.at[xc, yc]
                for n in range(1, 16):
                    self.send(spot, spot, 8, at_offset(x=n // 4, y=n % 4))
            else:
                self.all_of(8).wait_recv()

        def finish(self):
            for c in self.sends:
                c.wait_send()
            self.all_of(7).wait_send()
            self.all_of(8).wait_send()

    flows = [Flow(i) for i in range(len(FLOWS))]
    fc, fa = flows[0:1], flows[3:4]
    fd, fb = flows[1:3], flows[4:6]

    def step(*some):
        for group in some:
            for one in group:
                one.step()

    lax.fori_loop(0, 11, split_tap, 0)
    step(fc)
    for c in passing:
        c.wait_recv()
    puts = []

    def put(src, dst):
        c = pltpu.make_async_copy(src, dst, put_sem.at[len(puts)])
        c.start()
        puts.append(c)

    put(octin, octin_hbm)
    loads[3].wait()

    def turn(i, _):
        ot[:, pl.ds(pl.multiple_of(i * 384, 384), 384)] = (
            octin[pl.ds(6 * i, 6)].reshape(384, 256).T
        )
        return 0

    lax.fori_loop(0, 4, turn, 0)

    def down(i, _):
        rows = jnp.concatenate(
            [fine[:, 2 * i].reshape(1536, 128), fine[:, 2 * i + 1].reshape(1536, 128)], axis=1
        )
        grad = dot_nn(ot[...], rows).T.astype(BF)
        for c in range(2):
            one = grad[128 * c : 128 * c + 128]
            part[3, i, c, 1, 2:4] = one[0:32].reshape(2, 16, 256)
            part[3, i, c, 2] = one[32:96].reshape(4, 16, 256)
            part[3, i, c, 3, 0:2] = one[96:128].reshape(2, 16, 256)
        return 0

    lax.fori_loop(0, 4, down, 0)
    step(fd, fc)
    lax.fori_loop(0, 4, whole_tap(0), 0)
    step(fd)
    lax.fori_loop(4, 8, whole_tap(0), 0)
    step(fa, fc)
    lax.fori_loop(0, 4, whole_tap(1), 0)
    step(fa, fd, fc)
    lax.fori_loop(4, 8, whole_tap(1), 0)
    step(fb, fa, fd, fb, fc, fa, fd, fb, fc, fb, fa, fd, fb, fa, fb)

    k = dp
    lead = (27 * k + 7) // 8 * 8 - 27 * k
    start = pl.multiple_of(lead * 32, 32)
    conv[pl.ds(start, 256)] = red[0].reshape(256, 256)
    conv[pl.ds(start + 256, 256)] = red[1].reshape(256, 256)
    for n in range(11):
        row = 32 * (n + jnp.where(n < lead, 0, 16))
        piece = red[2 + n // 8, n % 8 // 2, (n % 2) * 2 : (n % 2) * 2 + 2]
        conv[pl.ds(pl.multiple_of(row, 32), 32)] = piece.reshape(32, 256)
    conv[864:896] = red[3, 1, 2:4].reshape(32, 256)
    conv[896:960] = red[3, 2].reshape(64, 256)
    conv[960:992] = red[3, 3, 0:2].reshape(32, 256)
    put(conv.at[0:864], conv_hbm)
    put(conv.at[864:992], down_hbm)
    for c in halos + passing:
        c.wait_send()
    for one in flows:
        one.finish()
    for c in puts:
        c.wait()


def final(scale, octin, dw, conv_in, down_in, fg, conv, down):
    res = dot_nt(octin[...].reshape(256, 256), dw[...]).astype(BF)
    for q in range(8):
        fg[:, q] = res[:, 128 * q : 128 * q + 128].reshape(4, 64, 128)
    conv[...] = conv_in[...].astype(F32) * scale
    down[...] = down_in[...].astype(F32) * scale


def body(grad_out, pre_act, conv_weight, down_weight, fine_act, neighbours, octant_routes):
    slots, voxels, channels = grad_out.shape[1:]
    any_space = pl.BlockSpec(memory_space=pl.ANY)
    smem = pl.BlockSpec(memory_space=pltpu.SMEM)
    V = pltpu.VMEM
    octin, conv, down = pl.pallas_call(
        kernel,
        out_shape=(
            jax.ShapeDtypeStruct((24, 64, 256), BF),
            jax.ShapeDtypeStruct((864, 256), BF),
            jax.ShapeDtypeStruct((128, 256), BF),
        ),
        in_specs=[smem, smem] + [any_space] * 4,
        out_specs=(any_space, any_space, any_space),
        scratch_shapes=[
            V((CAP + 1, 8, 64, 256), BF),
            V((CAP + 1, 8, 64, 256), BF),
            V((2, CAP + 1, 64, 256), BF),
            V((2, CAP + 1, 64, 256), BF),
            V((9, 10, 192, 256), BF),
            V((9, 10, 192, 256), BF),
            V((256, 1536), BF),
            V((27, 256, 256), BF),
            V((24, 8, 64, 128), BF),
            V((2, 768, 256), F32),
            V((25, 64, 256), BF),
            V((2, 8, 64, 256), BF),
            V((24, 64, 256), BF),
            V((256, 1536), BF),
            V((GROUPS, 4, 2, 4, 4, 16, 256), BF),
            V((GROUPS, 4, 4, 4, 16, 256), BF),
            V((GROUPS, 4, 4, 4, 16, 256), BF),
            V((GROUPS, 6, 2, 4, 16, 256), BF),
            V((GROUPS, 2, 2, 4, 16, 256), BF),
            V((GROUPS, 4, 4, 16, 256), BF),
            V((GROUPS, 15, 16, 256), BF),
            V((GROUPS, 4, 4, 16, 256), BF),
            V((992, 256), BF),
            pltpu.SemaphoreType.DMA((4,)),
            pltpu.SemaphoreType.DMA((4,)),
            pltpu.SemaphoreType.DMA((4,)),
            pltpu.SemaphoreType.DMA((4,)),
            pltpu.SemaphoreType.DMA((4,)),
            pltpu.SemaphoreType.DMA((len(FLOWS), 9)),
            pltpu.SemaphoreType.DMA((len(FLOWS), 9)),
            pltpu.SemaphoreType.DMA((3,)),
        ],
        compiler_params=pltpu.CompilerParams(
            collective_id=0, has_side_effects=True, vmem_limit_bytes=60 * 1024 * 1024
        ),
        name="backward",
    )(
        neighbours.transpose(1, 0, 2),
        octant_routes.transpose(0, 2, 1, 3),
        grad_out[0].reshape(slots, 8, 64, channels),
        pre_act[0].reshape(slots, 8, 64, channels),
        conv_weight,
        fine_act[0].reshape(24, 8, 64, 128),
    )
    factor = 1.0 / math.sqrt(lax.axis_size("dp") * lax.axis_size("dom") * slots * voxels)
    whole = pl.BlockSpec((128, 256), lambda i: (0, 0))
    rows = pl.BlockSpec((144, 256), lambda i: (i, 0))
    fg, conv, down = pl.pallas_call(
        lambda *refs: final(factor, *refs),
        out_shape=(
            jax.ShapeDtypeStruct((24, 8, 64, 128), BF),
            jax.ShapeDtypeStruct((864, 256), F32),
            jax.ShapeDtypeStruct((128, 256), F32),
        ),
        grid=(6,),
        in_specs=[
            pl.BlockSpec((4, 64, 256), lambda i: (i, 0, 0)),
            pl.BlockSpec((1024, 256), lambda i: (0, 0)),
            rows,
            whole,
        ],
        out_specs=(pl.BlockSpec((4, 8, 64, 128), lambda i: (i, 0, 0, 0)), rows, whole),
        name="final",
    )(octin, down_weight.reshape(1024, 256), conv, down)
    return (fg.reshape(fine_act.shape), conv, down)


def solution(mesh):
    return jax.shard_map(
        body,
        mesh=mesh,
        in_specs=(
            P("dp", "dom", None, None),
            P("dp", "dom", None, None),
            P(),
            P(),
            P("dp", "dom", None, None),
            P("dp", "dom", None),
            P("dp", "dom", None, None),
        ),
        out_specs=(P("dp", "dom", None, None), P("dp", None), P("dp", None)),
        check_vma=False,
    )
```

```python
import functools
import math

import jax
import jax.numpy as jnp
from jax import lax
from jax.experimental import pallas as pl
from jax.experimental.pallas import tpu as pltpu
from jax.sharding import PartitionSpec as P

MESH = pl.DeviceIdType.MESH
BF = jnp.bfloat16
F32 = jnp.float32
CAP = 3
GROUPS = 4
FLOWS = (
    (2, 0, 256, "z"),
    (3, 0, 128, "y"),
    (0, 0, 256, "x"),
    (1, 0, 128, "y"),
    (1, 128, 128, "z"),
    (3, 128, 128, "x"),
)
SPLIT = (9, 10, 13, 16, 2, 3, 6, 19, 20, 23, 26)


def dot_nt(a, b):
    return lax.dot_general(a, b, (((1,), (1,)), ((), ())), preferred_element_type=F32)


def dot_nn(a, b):
    return lax.dot_general(a, b, (((1,), (0,)), ((), ())), preferred_element_type=F32)


def kernel(
    scale, links, routes, g_hbm, p_hbm, w_hbm, dw_hbm, fine_hbm,
    fg, conv, down_out,
    g, p, face, pface, gsh, ash, gt, w, dw, fine, acc, octs, out, octin, ot,
    part, rcore, racc, r1, s1, a1, r2, red,
    load_sem, halo_s, halo_r, oct_s, oct_r, red_s, red_r,
):
    dp = lax.axis_index("dp")
    dom = lax.axis_index("dom")
    zc, cc = dp // 2, dp % 2
    yc, xc = dom // 4, dom % 4
    coord = {"z": zc, "x": xc, "y": yc}

    def at_offset(**offsets):
        z, x, y = (lax.rem(coord[a] + offsets.get(a, 0), 4) for a in "zxy")
        return (z * 2 + cc, y * 4 + x)

    partner = (zc * 2 + (1 - cc), dom)
    nxt = (dp, lax.rem(dom + 1, 16))
    prv = (dp, lax.rem(dom + 15, 16))

    barrier = pltpu.get_barrier_semaphore()
    peers = [partner, nxt, prv]
    for z in range(4):
        for x in range(4):
            for y in range(4):
                if (z, x, y) != (0, 0, 0) and 0 in (z, x, y):
                    peers.append(at_offset(z=z, x=x, y=y))
    for peer in peers:
        pl.semaphore_signal(barrier, inc=1, device_id=peer, device_id_type=MESH)

    loads = []
    for i, (src, dst) in enumerate(
        ((g_hbm, g.at[0:CAP]), (p_hbm, p.at[0:CAP]), (w_hbm, w), (fine_hbm, fine), (dw_hbm, dw))
    ):
        c = pltpu.make_async_copy(src, dst, load_sem.at[i])
        c.start()
        loads.append(c)
    g[CAP] = jnp.zeros(g.shape[1:], BF)
    p[CAP] = jnp.zeros(p.shape[1:], BF)
    for i in range(2):
        face[i, CAP] = jnp.zeros(face.shape[2:], BF)
        pface[i, CAP] = jnp.zeros(face.shape[2:], BF)
    octs[24] = jnp.zeros(octs.shape[1:], BF)
    for s in range(8):
        part[3, s // 2, s % 2, 3, :, :, 0:128] = jnp.zeros((4, 16, 128), BF)
    loads[0].wait()
    loads[1].wait()

    def rcopy(src, dst, ss, rs, to):
        return pltpu.make_async_remote_copy(
            src_ref=src, dst_ref=dst, send_sem=ss, recv_sem=rs, device_id=to, device_id_type=MESH
        )

    zi = lax.broadcasted_iota(jnp.int32, (10, 8, 256), 1)

    def expand(load, a, blk, plane, dst, relu):
        def slot(b, c):
            n = links[blk, 0, 9 * (a + 1) + 3 * (b + 1) + (c + 1)]
            return jnp.where(n < 0, CAP, n)

        cols = []
        for c in (-1, 0, 1):
            low = load(slot(-1, c), pl.ds(48, 16)).astype(F32)[8:16]
            mid = load(slot(0, c), pl.ds(0, 64)).astype(F32)
            high = load(slot(1, c), pl.ds(0, 16)).astype(F32)[0:8]
            col = jnp.concatenate([low, mid, high], axis=0)
            if relu:
                col = jnp.maximum(col, 0.0)
            cols.append(col.reshape(10, 8, 256))
        shifted = (
            pltpu.roll(jnp.where(zi == 7, cols[0], cols[1]), 1, 1),
            cols[1],
            pltpu.roll(jnp.where(zi == 0, cols[2], cols[1]), 7, 1),
        )
        rows = pl.ds(pl.multiple_of(blk * 64, 64), 64)
        for ty in range(3):
            for tz in range(3):
                dst[3 * ty + tz, plane, rows] = shifted[tz][ty : ty + 8].reshape(64, 256).astype(BF)

    def inner_g(n, _):
        blk, x = n // 8, n % 8
        expand(lambda s, r: g[s, x, r], 0, blk, x + 1, gsh, False)
        return 0

    def outer_g(blk, _):
        expand(lambda s, r: face[0, s, r], -1, blk, 0, gsh, False)
        expand(lambda s, r: face[1, s, r], 1, blk, 9, gsh, False)
        return 0

    def inner_p(n, _):
        blk, x = n // 8, n % 8
        expand(lambda s, r: p[s, x, r], 0, blk, x + 1, ash, True)
        return 0

    def outer_p(blk, _):
        expand(lambda s, r: pface[0, s, r], -1, blk, 0, ash, True)
        expand(lambda s, r: pface[1, s, r], 1, blk, 9, ash, True)
        return 0

    def input_grad(half, first, last):
        def taps(n, _):
            tx, ty = n // 3, n % 3
            lhs = jnp.concatenate(
                [
                    gsh[8 - 3 * ty - tz, pl.ds(2 - tx + 4 * half, 4)].reshape(768, 256)
                    for tz in range(3)
                ],
                axis=1,
            )
            rhs = jnp.concatenate([w[3 * n + tz] for tz in range(3)], axis=1)
            acc[half] += dot_nt(lhs, rhs)
            return 0

        lax.fori_loop(first, last, taps, 0)

    lower = lax.broadcasted_iota(jnp.int32, (2, 8, 256), 1) < 4

    def octants(half):
        def plane(n, _):
            cx, blk = n // CAP, n % CAP
            val = acc[half, pl.ds(pl.multiple_of(n * 64, 64), 64)]
            pre = p[blk, 4 * half + cx].astype(F32)
            val = jnp.where(pre > 0.0, val, 0.0).reshape(2, 2, 2, 8, 256)
            for oy in range(2):
                even, odd = val[oy, :, 0], val[oy, :, 1]
                first = jnp.where(lower, even, pltpu.roll(odd, 4, 1))
                second = jnp.where(lower, pltpu.roll(even, 4, 1), odd)
                rows = pl.ds(pl.multiple_of(cx * 16, 16), 16)
                slot = blk * 8 + 4 * half + 2 * oy
                octs[slot, rows] = first.reshape(16, 256).astype(BF)
                octs[slot + 1, rows] = second.reshape(16, 256).astype(BF)
            return 0

        lax.fori_loop(0, 4 * CAP, plane, 0)

    passing = []

    def route(half):
        def place(k):
            def one(j, _):
                e = routes[0, k, 0, j]
                val = octs[jnp.where(e < 0, 24, e)]
                if k == 1:
                    octin[8 + j] = val
                else:
                    out[k // 2, j] = val
                return 0

            lax.fori_loop(4 * half, 4 * half + 4, one, 0)

        place(0)
        place(2)
        for k, base, to in ((0, 0, prv), (1, 16, nxt)):
            i = 2 * half + k
            c = rcopy(
                out.at[k, 4 * half : 4 * half + 4],
                octin.at[base + 4 * half : base + 4 * half + 4],
                oct_s.at[i], oct_r.at[i], to,
            )
            c.start()
            passing.append(c)
        place(1)

    lax.fori_loop(0, CAP * 8, inner_p, 0)
    pl.semaphore_wait(barrier, len(peers))

    halos = []
    for i, (src, dst, to) in enumerate(
        (
            (p.at[0:CAP, 7], pface.at[0], nxt),
            (p.at[0:CAP, 0], pface.at[1], prv),
            (g.at[0:CAP, 7], face.at[0], nxt),
            (g.at[0:CAP, 0], face.at[1], prv),
        )
    ):
        c = rcopy(src, dst.at[0:CAP], halo_s.at[i], halo_r.at[i], to)
        c.start()
        halos.append(c)

    lax.fori_loop(0, CAP * 8, inner_g, 0)
    acc[...] = jnp.zeros(acc.shape, F32)

    def transpose_plane(x, _):
        gt[:, pl.ds(pl.multiple_of(x * 384, 384), 384)] = (
            gsh[4, pl.ds(1 + 2 * x, 2)].reshape(384, 256).T
        )
        return 0

    lax.fori_loop(0, 4, transpose_plane, 0)

    def tap(t):
        tx, tyz = t // 9, t % 9
        rows = ash[tyz, pl.ds(tx, 8)].reshape(1536, 256)
        return dot_nn(gt[...], rows).T.astype(BF)

    def whole_tap(shift):
        def one(k, _):
            part[shift, k // 2, k % 2] = tap((27 * k + 7) // 8 + shift).reshape(4, 4, 16, 256)
            return 0

        return one

    def split_tap(t):
        grad = tap(t)
        for i in range(8):
            k, r = divmod(8 * t + i, 27)
            pos = r if t < (27 * k + 7) // 8 else r - 16
            rows = grad[32 * i : 32 * i + 32]
            if pos < 8:
                y = pos % 2 * 2
                part[2, k // 2, k % 2, pos // 2, y : y + 2] = rows.reshape(2, 16, 256)
            else:
                for n in range(4):
                    part[3, k // 2, k % 2, pos - 8, n, :, 0:128] = rows[
                        n // 2 * 16 : n // 2 * 16 + 16, n % 2 * 128 : n % 2 * 128 + 128
                    ]

    def cut(ref, axis, at):
        return ref.at[tuple(at if d == axis else slice(None) for d in "zxy")]

    class Flow:
        def __init__(self, n):
            self.n = n
            grp, lane, width, self.axis = FLOWS[n]
            lanes = pl.ds(lane, width)
            self.part = part.at[grp, :, :, :, :, :, lanes]
            self.rcore = rcore.at[grp, :, :, :, :, lanes]
            self.racc = racc.at[grp, :, :, :, :, lanes]
            self.r1 = r1.at[grp, :, :, :, :, lanes]
            self.s1 = s1.at[grp, :, :, :, :, lanes]
            self.a1 = a1.at[grp, :, :, :, lanes]
            self.r2 = r2.at[grp, :, :, lanes]
            self.red = red.at[grp, :, :, :, lanes]
            self.stage = 0
            self.sends = []

        def send(self, src, dst, i, to):
            c = rcopy(src, dst, red_s.at[self.n, i], red_r.at[self.n, i], to)
            c.start()
            if i < 7:
                self.sends.append(c)
            return c

        def all_of(self, i):
            return rcopy(self.r2, self.r2, red_s.at[self.n, i], red_r.at[self.n, i], partner)

        def chunk(self, off, half):
            ref = cut(self.racc, self.axis, lax.rem(coord[self.axis] + off, 4))
            return ref.at[2 * half : 2 * half + 2]

        def step(self):
            axis = self.axis
            left, right = at_offset(**{axis: 3}), at_offset(**{axis: 1})
            u, v = "zxy".replace(axis, "")
            stage = self.stage
            self.stage += 1
            if stage == 0:
                self.core = self.send(self.part.at[:, 1 - cc], self.rcore, 0, partner)
            elif stage == 1:
                self.core.wait_recv()
                for z in range(4):
                    self.racc[z] = (
                        self.part[z, cc].astype(F32) + self.rcore[z].astype(F32)
                    ).astype(BF)
                box = self.r1
                self.relay_a = self.send(self.chunk(2, 0), box.at[0], 1, right)
                self.relay_b = self.send(self.chunk(2, 1), box.at[1], 2, left)
                self.direct_b = self.send(self.chunk(1, 1), box.at[2], 3, right)
                self.direct_a = self.send(self.chunk(3, 0), box.at[3], 4, left)
            elif stage == 2:
                box = self.r1
                self.relay_a.wait_recv()
                self.s1[0] = (self.chunk(1, 0)[...].astype(F32) + box[0].astype(F32)).astype(BF)
                self.sum_a = self.send(self.s1.at[0], box.at[4], 5, right)
                self.relay_b.wait_recv()
                self.s1[1] = (self.chunk(3, 1)[...].astype(F32) + box[1].astype(F32)).astype(BF)
                self.sum_b = self.send(self.s1.at[1], box.at[5], 6, left)
            elif stage == 3:
                for c in (self.direct_a, self.direct_b, self.sum_a, self.sum_b):
                    c.wait_recv()
                for half, (i, j) in enumerate(((4, 3), (5, 2))):
                    total = self.chunk(0, half)[...].astype(F32)
                    total = total + self.r1[i].astype(F32) + self.r1[j].astype(F32)
                    self.a1[2 * half : 2 * half + 2] = total.astype(BF)
                for n in range(1, 16):
                    du, dv = n // 4, n % 4
                    src = self.a1.at[lax.rem(coord[u] + du, 4), lax.rem(coord[v] + dv, 4)]
                    self.send(src, self.r2.at[n - 1], 7, at_offset(**{u: du, v: dv}))
            elif stage == 4:
                self.all_of(7).wait_recv()
                total = self.a1[coord[u], coord[v]].astype(F32)
                for n in range(15):
                    total = total + self.r2[n].astype(F32)
                self.red[xc, yc] = total.astype(BF)
                spot = self.red.at[xc, yc]
                for n in range(1, 16):
                    self.send(spot, spot, 8, at_offset(x=n // 4, y=n % 4))
            else:
                self.all_of(8).wait_recv()

        def finish(self):
            for c in self.sends:
                c.wait_send()
            self.all_of(7).wait_send()
            self.all_of(8).wait_send()

    flows = [Flow(i) for i in range(len(FLOWS))]
    fc, fa, fb, fd = flows[0:2], flows[2:3], flows[3:5], flows[5:6]

    def step(*some):
        for group in some:
            for one in group:
                one.step()

    for t in SPLIT[:4]:
        split_tap(t)
    halos[0].wait_recv()
    halos[1].wait_recv()
    lax.fori_loop(0, CAP, outer_p, 0)
    for t in SPLIT[4:]:
        split_tap(t)
    step(fc)
    lax.fori_loop(0, 8, whole_tap(0), 0)
    step(fa, fc)
    halos[2].wait_recv()
    halos[3].wait_recv()
    lax.fori_loop(0, CAP, outer_g, 0)
    loads[2].wait()
    input_grad(0, 0, 5)
    step(fa, fc)
    input_grad(0, 5, 9)
    octants(0)
    route(0)
    step(fa, fc)
    input_grad(1, 0, 5)
    step(fa, fc)
    input_grad(1, 5, 9)
    octants(1)
    route(1)
    step(fa, fc)
    lax.fori_loop(0, 8, whole_tap(1), 0)
    step(fb, fa)
    loads[4].wait()

    def fine_grad(i, _):
        at = pl.ds(4 * i, 4)
        res = dot_nt(octin[at].reshape(256, 256), dw[...]).astype(BF)
        for q in range(8):
            fg[at, q] = res[:, 128 * q : 128 * q + 128].reshape(4, 64, 128)
        return 0

    lax.fori_loop(2, 4, fine_grad, 0)
    loads[3].wait()
    step(fb)
    for c in passing:
        c.wait_recv()

    def turn(i, _):
        ot[:, pl.ds(pl.multiple_of(i * 384, 384), 384)] = (
            octin[pl.ds(6 * i, 6)].reshape(384, 256).T
        )
        return 0

    lax.fori_loop(0, 4, turn, 0)

    def down(i, _):
        rows = jnp.concatenate(
            [fine[:, 2 * i].reshape(1536, 128), fine[:, 2 * i + 1].reshape(1536, 128)], axis=1
        )
        grad = dot_nn(ot[...], rows).T.astype(BF)
        for c in range(2):
            one = grad[128 * c : 128 * c + 128]
            for n in range(16):
                part[3, i, c, n // 4, n % 4, :, 128:256] = one[
                    n // 2 * 16 : n // 2 * 16 + 16, n % 2 * 128 : n % 2 * 128 + 128
                ]
        return 0

    lax.fori_loop(0, 4, down, 0)
    step(fd, fb)

    lead = (27 * dp + 7) // 8 * 8 - 27 * dp
    start = pl.multiple_of(lead * 32, 32)

    def finished(value):
        return value.astype(F32) * scale

    conv[pl.ds(start, 256)] = finished(red[0].reshape(256, 256))
    for n in range(11):
        row = pl.multiple_of(32 * (n + jnp.where(n < lead, 0, 16)), 32)
        if n < 8:
            piece = red[2, n // 2, (n % 2) * 2 : (n % 2) * 2 + 2]
            conv[pl.ds(row, 32)] = finished(piece.reshape(32, 256))
        else:
            for m in range(4):
                conv[pl.ds(row + m // 2 * 16, 16), m % 2 * 128 : m % 2 * 128 + 128] = finished(
                    red[3, n - 8, m, :, 0:128]
                )
    lax.fori_loop(0, 2, fine_grad, 0)
    step(fd, fb)
    lax.fori_loop(4, 6, fine_grad, 0)
    step(fd, fb, fd, fb, fd)
    conv[pl.ds(start + 256, 256)] = finished(red[1].reshape(256, 256))
    step(fd)
    for n in range(16):
        down_out[n // 2 * 16 : n // 2 * 16 + 16, n % 2 * 128 : n % 2 * 128 + 128] = finished(
            red[3, n // 4, n % 4, :, 128:256]
        )
    for c in halos + passing:
        c.wait_send()
    for one in flows:
        one.finish()


def body(grad_out, pre_act, conv_weight, down_weight, fine_act, neighbours, octant_routes):
    slots, voxels, channels = grad_out.shape[1:]
    any_space = pl.BlockSpec(memory_space=pl.ANY)
    smem = pl.BlockSpec(memory_space=pltpu.SMEM)
    V = pltpu.VMEM
    factor = 1.0 / math.sqrt(lax.axis_size("dp") * lax.axis_size("dom") * slots * voxels)
    vmem = pl.BlockSpec(memory_space=V)
    fg, conv, down = pl.pallas_call(
        functools.partial(kernel, factor),
        out_shape=(V((24, 8, 64, 128), BF), V((864, 256), F32), V((128, 256), F32)),
        in_specs=[smem, smem] + [any_space] * 5,
        out_specs=(vmem, vmem, vmem),
        scratch_shapes=[
            V((CAP + 1, 8, 64, 256), BF),
            V((CAP + 1, 8, 64, 256), BF),
            V((2, CAP + 1, 64, 256), BF),
            V((2, CAP + 1, 64, 256), BF),
            V((9, 10, 192, 256), BF),
            V((9, 10, 192, 256), BF),
            V((256, 1536), BF),
            V((27, 256, 256), BF),
            V((1024, 256), BF),
            V((24, 8, 64, 128), BF),
            V((2, 768, 256), F32),
            V((25, 64, 256), BF),
            V((2, 8, 64, 256), BF),
            V((24, 64, 256), BF),
            V((256, 1536), BF),
            V((GROUPS, 4, 2, 4, 4, 16, 256), BF),
            V((GROUPS, 4, 4, 4, 16, 256), BF),
            V((GROUPS, 4, 4, 4, 16, 256), BF),
            V((GROUPS, 6, 2, 4, 16, 256), BF),
            V((GROUPS, 2, 2, 4, 16, 256), BF),
            V((GROUPS, 4, 4, 16, 256), BF),
            V((GROUPS, 15, 16, 256), BF),
            V((GROUPS, 4, 4, 16, 256), BF),
            pltpu.SemaphoreType.DMA((5,)),
            pltpu.SemaphoreType.DMA((4,)),
            pltpu.SemaphoreType.DMA((4,)),
            pltpu.SemaphoreType.DMA((4,)),
            pltpu.SemaphoreType.DMA((4,)),
            pltpu.SemaphoreType.DMA((len(FLOWS), 9)),
            pltpu.SemaphoreType.DMA((len(FLOWS), 9)),
        ],
        compiler_params=pltpu.CompilerParams(
            collective_id=0, has_side_effects=True, vmem_limit_bytes=54 * 1024 * 1024
        ),
        name="backward",
    )(
        neighbours.transpose(1, 0, 2),
        octant_routes.transpose(0, 2, 1, 3),
        grad_out[0].reshape(slots, 8, 64, channels),
        pre_act[0].reshape(slots, 8, 64, channels),
        conv_weight,
        down_weight.reshape(1024, 256),
        fine_act[0].reshape(24, 8, 64, 128),
    )
    return (fg.reshape(fine_act.shape), conv, down)


def solution(mesh):
    return jax.shard_map(
        body,
        mesh=mesh,
        in_specs=(
            P("dp", "dom", None, None),
            P("dp", "dom", None, None),
            P(),
            P(),
            P("dp", "dom", None, None),
            P("dp", "dom", None),
            P("dp", "dom", None, None),
        ),
        out_specs=(P("dp", "dom", None, None), P("dp", None), P("dp", None)),
        check_vma=False,
    )
```

```python
import functools
import math

import jax
import jax.numpy as jnp
from jax import lax
from jax.experimental import pallas as pl
from jax.experimental.pallas import tpu as pltpu
from jax.sharding import PartitionSpec as P

MESH = pl.DeviceIdType.MESH
BF = jnp.bfloat16
F32 = jnp.float32
CAP = 3
GROUPS = 4
FLOWS = (
    (2, 0, 256, "z"),
    (3, 0, 128, "y"),
    (0, 0, 256, "z"),
    (1, 0, 128, "y"),
    (1, 128, 128, "z"),
    (3, 128, 128, "x"),
)
SPLIT = (9, 10, 13, 16, 2, 3, 6, 19, 20, 23, 26)


def dot_nt(a, b):
    return lax.dot_general(a, b, (((1,), (1,)), ((), ())), preferred_element_type=F32)


def dot_nn(a, b):
    return lax.dot_general(a, b, (((1,), (0,)), ((), ())), preferred_element_type=F32)


def kernel(
    scale, links, routes, g_hbm, p_hbm, w_hbm, dw_hbm, fine_hbm,
    fg, conv, down_out,
    g, p, face, pface, gsh, ash, gt, w, dw, fine, acc, octs, out, octin, ot,
    part, rcore, racc, r1, a1, r2, red,
    load_sem, halo_s, halo_r, oct_s, oct_r, red_s, red_r,
):
    dp = lax.axis_index("dp")
    dom = lax.axis_index("dom")
    zc, cc = dp // 2, dp % 2
    yc, xc = dom // 4, dom % 4
    coord = {"z": zc, "x": xc, "y": yc}

    def at_offset(**offsets):
        z, x, y = (lax.rem(coord[a] + offsets.get(a, 0), 4) for a in "zxy")
        return (z * 2 + cc, y * 4 + x)

    partner = (zc * 2 + (1 - cc), dom)
    nxt = (dp, lax.rem(dom + 1, 16))
    prv = (dp, lax.rem(dom + 15, 16))

    barrier = pltpu.get_barrier_semaphore()
    peers = [partner, nxt, prv]
    for z in range(4):
        for x in range(4):
            for y in range(4):
                if (z, x, y) != (0, 0, 0) and 0 in (z, x, y):
                    peers.append(at_offset(z=z, x=x, y=y))
    for peer in peers:
        pl.semaphore_signal(barrier, inc=1, device_id=peer, device_id_type=MESH)

    loads = []
    for i, (src, dst) in enumerate(
        ((g_hbm, g.at[0:CAP]), (p_hbm, p.at[0:CAP]), (w_hbm, w), (fine_hbm, fine), (dw_hbm, dw))
    ):
        c = pltpu.make_async_copy(src, dst, load_sem.at[i])
        c.start()
        loads.append(c)
    g[CAP] = jnp.zeros(g.shape[1:], BF)
    p[CAP] = jnp.zeros(p.shape[1:], BF)
    for i in range(2):
        face[i, CAP] = jnp.zeros(face.shape[2:], BF)
        pface[i, CAP] = jnp.zeros(face.shape[2:], BF)
    octs[24] = jnp.zeros(octs.shape[1:], BF)
    for s in range(8):
        part[3, s // 2, s % 2, 3, :, :, 0:128] = jnp.zeros((4, 16, 128), BF)
    loads[0].wait()
    loads[1].wait()

    def rcopy(src, dst, ss, rs, to):
        return pltpu.make_async_remote_copy(
            src_ref=src, dst_ref=dst, send_sem=ss, recv_sem=rs, device_id=to, device_id_type=MESH
        )

    zi = lax.broadcasted_iota(jnp.int32, (10, 8, 256), 1)

    def expand(load, a, blk, plane, dst, relu):
        def slot(b, c):
            n = links[blk, 0, 9 * (a + 1) + 3 * (b + 1) + (c + 1)]
            return jnp.where(n < 0, CAP, n)

        cols = []
        for c in (-1, 0, 1):
            low = load(slot(-1, c), pl.ds(48, 16)).astype(F32)[8:16]
            mid = load(slot(0, c), pl.ds(0, 64)).astype(F32)
            high = load(slot(1, c), pl.ds(0, 16)).astype(F32)[0:8]
            col = jnp.concatenate([low, mid, high], axis=0)
            if relu:
                col = jnp.maximum(col, 0.0)
            cols.append(col.reshape(10, 8, 256))
        shifted = (
            pltpu.roll(jnp.where(zi == 7, cols[0], cols[1]), 1, 1),
            cols[1],
            pltpu.roll(jnp.where(zi == 0, cols[2], cols[1]), 7, 1),
        )
        rows = pl.ds(pl.multiple_of(blk * 64, 64), 64)
        for ty in range(3):
            for tz in range(3):
                dst[3 * ty + tz, plane, rows] = shifted[tz][ty : ty + 8].reshape(64, 256).astype(BF)

    def inner_g(n, _):
        blk, x = n // 8, n % 8
        expand(lambda s, r: g[s, x, r], 0, blk, x + 1, gsh, False)
        return 0

    def outer_g(blk, _):
        expand(lambda s, r: face[0, s, r], -1, blk, 0, gsh, False)
        expand(lambda s, r: face[1, s, r], 1, blk, 9, gsh, False)
        return 0

    def inner_p(n, _):
        blk, x = n // 8, n % 8
        expand(lambda s, r: p[s, x, r], 0, blk, x + 1, ash, True)
        return 0

    def outer_p(blk, _):
        expand(lambda s, r: pface[0, s, r], -1, blk, 0, ash, True)
        expand(lambda s, r: pface[1, s, r], 1, blk, 9, ash, True)
        return 0

    def input_grad(half, first, last):
        def taps(n, _):
            tx, ty = n // 3, n % 3
            lhs = jnp.concatenate(
                [
                    gsh[8 - 3 * ty - tz, pl.ds(2 - tx + 4 * half, 4)].reshape(768, 256)
                    for tz in range(3)
                ],
                axis=1,
            )
            rhs = jnp.concatenate([w[3 * n + tz] for tz in range(3)], axis=1)
            acc[half] += dot_nt(lhs, rhs)
            return 0

        lax.fori_loop(first, last, taps, 0)

    lower = lax.broadcasted_iota(jnp.int32, (2, 8, 256), 1) < 4

    def octants(half):
        def plane(n, _):
            cx, blk = n // CAP, n % CAP
            val = acc[half, pl.ds(pl.multiple_of(n * 64, 64), 64)]
            pre = p[blk, 4 * half + cx].astype(F32)
            val = jnp.where(pre > 0.0, val, 0.0).reshape(2, 2, 2, 8, 256)
            for oy in range(2):
                even, odd = val[oy, :, 0], val[oy, :, 1]
                first = jnp.where(lower, even, pltpu.roll(odd, 4, 1))
                second = jnp.where(lower, pltpu.roll(even, 4, 1), odd)
                rows = pl.ds(pl.multiple_of(cx * 16, 16), 16)
                slot = blk * 8 + 4 * half + 2 * oy
                octs[slot, rows] = first.reshape(16, 256).astype(BF)
                octs[slot + 1, rows] = second.reshape(16, 256).astype(BF)
            return 0

        lax.fori_loop(0, 4 * CAP, plane, 0)

    passing = []

    def route(half):
        def place(k):
            def one(j, _):
                e = routes[0, k, 0, j]
                val = octs[jnp.where(e < 0, 24, e)]
                if k == 1:
                    octin[8 + j] = val
                else:
                    out[k // 2, j] = val
                return 0

            lax.fori_loop(4 * half, 4 * half + 4, one, 0)

        place(0)
        place(2)
        for k, base, to in ((0, 0, prv), (1, 16, nxt)):
            i = 2 * half + k
            c = rcopy(
                out.at[k, 4 * half : 4 * half + 4],
                octin.at[base + 4 * half : base + 4 * half + 4],
                oct_s.at[i], oct_r.at[i], to,
            )
            c.start()
            passing.append(c)
        place(1)

    lax.fori_loop(0, CAP * 8, inner_p, 0)
    pl.semaphore_wait(barrier, len(peers))

    halos = []
    for i, (src, dst, to) in enumerate(
        (
            (p.at[0:CAP, 7], pface.at[0], nxt),
            (p.at[0:CAP, 0], pface.at[1], prv),
            (g.at[0:CAP, 7], face.at[0], nxt),
            (g.at[0:CAP, 0], face.at[1], prv),
        )
    ):
        c = rcopy(src, dst.at[0:CAP], halo_s.at[i], halo_r.at[i], to)
        c.start()
        halos.append(c)

    lax.fori_loop(0, CAP * 8, inner_g, 0)
    acc[...] = jnp.zeros(acc.shape, F32)

    def transpose_plane(x, _):
        gt[:, pl.ds(pl.multiple_of(x * 384, 384), 384)] = (
            gsh[4, pl.ds(1 + 2 * x, 2)].reshape(384, 256).T
        )
        return 0

    lax.fori_loop(0, 4, transpose_plane, 0)

    def tap(t):
        tx, tyz = t // 9, t % 9
        rows = ash[tyz, pl.ds(tx, 8)].reshape(1536, 256)
        return dot_nn(gt[...], rows).T.astype(BF)

    def whole_tap(shift):
        def one(k, _):
            part[shift, k // 2, k % 2] = tap((27 * k + 7) // 8 + shift).reshape(4, 4, 16, 256)
            return 0

        return one

    def split_tap(t):
        grad = tap(t)
        for i in range(8):
            k, r = divmod(8 * t + i, 27)
            pos = r if t < (27 * k + 7) // 8 else r - 16
            rows = grad[32 * i : 32 * i + 32]
            if pos < 8:
                y = pos % 2 * 2
                part[2, k // 2, k % 2, pos // 2, y : y + 2] = rows.reshape(2, 16, 256)
            else:
                for n in range(4):
                    part[3, k // 2, k % 2, pos - 8, n, :, 0:128] = rows[
                        n // 2 * 16 : n // 2 * 16 + 16, n % 2 * 128 : n % 2 * 128 + 128
                    ]

    def cut(ref, axis, at):
        return ref.at[tuple(at if d == axis else slice(None) for d in "zxy")]

    class Flow:
        def __init__(self, n):
            self.n = n
            grp, lane, width, self.axis = FLOWS[n]
            lanes = pl.ds(lane, width)
            self.part = part.at[grp, :, :, :, :, :, lanes]
            self.rcore = rcore.at[grp, :, :, :, :, lanes]
            self.racc = racc.at[grp, :, :, :, :, lanes]
            self.r1 = r1.at[grp, :, :, :, :, lanes]
            self.a1 = a1.at[grp, :, :, :, lanes]
            self.r2 = r2.at[grp, :, :, lanes]
            self.red = red.at[grp, :, :, :, lanes]
            self.stage = 0

        def send(self, src, dst, i, to):
            c = rcopy(src, dst, red_s.at[self.n, i], red_r.at[self.n, i], to)
            c.start()
            return c

        def all_of(self, i):
            ref = (self.rcore, self.r1, self.r2, self.r2)[i]
            return rcopy(ref, ref, red_s.at[self.n, i], red_r.at[self.n, i], partner)

        def chunk(self, off):
            return cut(self.racc, self.axis, lax.rem(coord[self.axis] + off, 4))

        def step(self):
            axis = self.axis
            u, v = "zxy".replace(axis, "")
            stage = self.stage
            self.stage += 1
            if stage > 0:
                self.all_of(stage - 1).wait_recv()
            if stage == 0:
                self.send(self.part.at[:, 1 - cc], self.rcore, 0, partner)
            elif stage == 1:
                for z in range(4):
                    self.racc[z] = (
                        self.part[z, cc].astype(F32) + self.rcore[z].astype(F32)
                    ).astype(BF)
                for off in (2, 1, 3):
                    self.send(self.chunk(off), self.r1.at[off - 1], 1, at_offset(**{axis: off}))
            elif stage == 2:
                total = self.chunk(0)[...].astype(F32)
                for n in range(3):
                    total = total + self.r1[n].astype(F32)
                self.a1[...] = total.astype(BF)
                for n in range(1, 16):
                    du, dv = n // 4, n % 4
                    src = self.a1.at[lax.rem(coord[u] + du, 4), lax.rem(coord[v] + dv, 4)]
                    self.send(src, self.r2.at[n - 1], 2, at_offset(**{u: du, v: dv}))
            elif stage == 3:
                total = self.a1[coord[u], coord[v]].astype(F32)
                for n in range(15):
                    total = total + self.r2[n].astype(F32)
                self.red[xc, yc] = total.astype(BF)
                spot = self.red.at[xc, yc]
                for n in range(1, 16):
                    self.send(spot, spot, 3, at_offset(x=n // 4, y=n % 4))

        def finish(self):
            for i in range(4):
                self.all_of(i).wait_send()

    flows = [Flow(i) for i in range(len(FLOWS))]
    fc, fa, fb, fd = flows[0:2], flows[2:3], flows[3:5], flows[5:6]

    def step(*some):
        for group in some:
            for one in group:
                one.step()

    for t in SPLIT[:4]:
        split_tap(t)
    halos[0].wait_recv()
    halos[1].wait_recv()
    lax.fori_loop(0, CAP, outer_p, 0)
    for t in SPLIT[4:]:
        split_tap(t)
    step(fc)
    halos[2].wait_recv()
    halos[3].wait_recv()
    lax.fori_loop(0, CAP, outer_g, 0)
    loads[2].wait()
    input_grad(0, 0, 5)
    step(fc)
    input_grad(0, 5, 9)
    octants(0)
    route(0)
    input_grad(1, 0, 9)
    octants(1)
    route(1)
    step(fc)
    lax.fori_loop(0, 8, whole_tap(0), 0)
    step(fa)
    lax.fori_loop(0, 8, whole_tap(1), 0)
    step(fb, fa, fc)
    loads[4].wait()

    def fine_grad(i, _):
        at = pl.ds(4 * i, 4)
        res = dot_nt(octin[at].reshape(256, 256), dw[...]).astype(BF)
        for q in range(8):
            fg[at, q] = res[:, 128 * q : 128 * q + 128].reshape(4, 64, 128)
        return 0

    lax.fori_loop(2, 4, fine_grad, 0)
    loads[3].wait()
    for c in passing:
        c.wait_recv()
    step(fb)

    def turn(i, _):
        ot[:, pl.ds(pl.multiple_of(i * 384, 384), 384)] = (
            octin[pl.ds(6 * i, 6)].reshape(384, 256).T
        )
        return 0

    lax.fori_loop(0, 4, turn, 0)

    def down(i, _):
        rows = jnp.concatenate(
            [fine[:, 2 * i].reshape(1536, 128), fine[:, 2 * i + 1].reshape(1536, 128)], axis=1
        )
        grad = dot_nn(ot[...], rows).T.astype(BF)
        for c in range(2):
            one = grad[128 * c : 128 * c + 128]
            for n in range(16):
                part[3, i, c, n // 4, n % 4, :, 128:256] = one[
                    n // 2 * 16 : n // 2 * 16 + 16, n % 2 * 128 : n % 2 * 128 + 128
                ]
        return 0

    lax.fori_loop(0, 4, down, 0)
    step(fd)
    lax.fori_loop(0, 2, fine_grad, 0)
    lax.fori_loop(4, 6, fine_grad, 0)
    step(fa, fc, fd)

    lead = (27 * dp + 7) // 8 * 8 - 27 * dp
    start = pl.multiple_of(lead * 32, 32)

    def finished(value):
        return value.astype(F32) * scale

    for n in range(11):
        row = pl.multiple_of(32 * (n + jnp.where(n < lead, 0, 16)), 32)
        if n < 8:
            piece = red[2, n // 2, (n % 2) * 2 : (n % 2) * 2 + 2]
            conv[pl.ds(row, 32)] = finished(piece.reshape(32, 256))
        else:
            for m in range(4):
                conv[pl.ds(row + m // 2 * 16, 16), m % 2 * 128 : m % 2 * 128 + 128] = finished(
                    red[3, n - 8, m, :, 0:128]
                )
    step(fb, fa, fd, fb, fa)
    conv[pl.ds(start, 256)] = finished(red[0].reshape(256, 256))
    step(fd, fb)
    conv[pl.ds(start + 256, 256)] = finished(red[1].reshape(256, 256))
    step(fd)
    for n in range(16):
        down_out[n // 2 * 16 : n // 2 * 16 + 16, n % 2 * 128 : n % 2 * 128 + 128] = finished(
            red[3, n // 4, n % 4, :, 128:256]
        )
    for c in halos + passing:
        c.wait_send()
    for one in flows:
        one.finish()


def body(grad_out, pre_act, conv_weight, down_weight, fine_act, neighbours, octant_routes):
    slots, voxels, channels = grad_out.shape[1:]
    any_space = pl.BlockSpec(memory_space=pl.ANY)
    smem = pl.BlockSpec(memory_space=pltpu.SMEM)
    V = pltpu.VMEM
    factor = 1.0 / math.sqrt(lax.axis_size("dp") * lax.axis_size("dom") * slots * voxels)
    vmem = pl.BlockSpec(memory_space=V)
    fg, conv, down = pl.pallas_call(
        functools.partial(kernel, factor),
        out_shape=(V((24, 8, 64, 128), BF), V((864, 256), F32), V((128, 256), F32)),
        in_specs=[smem, smem] + [any_space] * 5,
        out_specs=(vmem, vmem, vmem),
        scratch_shapes=[
            V((CAP + 1, 8, 64, 256), BF),
            V((CAP + 1, 8, 64, 256), BF),
            V((2, CAP + 1, 64, 256), BF),
            V((2, CAP + 1, 64, 256), BF),
            V((9, 10, 192, 256), BF),
            V((9, 10, 192, 256), BF),
            V((256, 1536), BF),
            V((27, 256, 256), BF),
            V((1024, 256), BF),
            V((24, 8, 64, 128), BF),
            V((2, 768, 256), F32),
            V((25, 64, 256), BF),
            V((2, 8, 64, 256), BF),
            V((24, 64, 256), BF),
            V((256, 1536), BF),
            V((GROUPS, 4, 2, 4, 4, 16, 256), BF),
            V((GROUPS, 4, 4, 4, 16, 256), BF),
            V((GROUPS, 4, 4, 4, 16, 256), BF),
            V((GROUPS, 3, 4, 4, 16, 256), BF),
            V((GROUPS, 4, 4, 16, 256), BF),
            V((GROUPS, 15, 16, 256), BF),
            V((GROUPS, 4, 4, 16, 256), BF),
            pltpu.SemaphoreType.DMA((5,)),
            pltpu.SemaphoreType.DMA((4,)),
            pltpu.SemaphoreType.DMA((4,)),
            pltpu.SemaphoreType.DMA((4,)),
            pltpu.SemaphoreType.DMA((4,)),
            pltpu.SemaphoreType.DMA((len(FLOWS), 4)),
            pltpu.SemaphoreType.DMA((len(FLOWS), 4)),
        ],
        compiler_params=pltpu.CompilerParams(
            collective_id=0, has_side_effects=True, vmem_limit_bytes=54 * 1024 * 1024
        ),
        name="backward",
    )(
        neighbours.transpose(1, 0, 2),
        octant_routes.transpose(0, 2, 1, 3),
        grad_out[0].reshape(slots, 8, 64, channels),
        pre_act[0].reshape(slots, 8, 64, channels),
        conv_weight,
        down_weight.reshape(1024, 256),
        fine_act[0].reshape(24, 8, 64, 128),
    )
    return (fg.reshape(fine_act.shape), conv, down)


def solution(mesh):
    return jax.shard_map(
        body,
        mesh=mesh,
        in_specs=(
            P("dp", "dom", None, None),
            P("dp", "dom", None, None),
            P(),
            P(),
            P("dp", "dom", None, None),
            P("dp", "dom", None),
            P("dp", "dom", None, None),
        ),
        out_specs=(P("dp", "dom", None, None), P("dp", None), P("dp", None)),
        check_vma=False,
    )
```

```python
import functools
import math

import jax
import jax.numpy as jnp
from jax import lax
from jax.experimental import pallas as pl
from jax.experimental.pallas import tpu as pltpu
from jax.sharding import PartitionSpec as P

MESH = pl.DeviceIdType.MESH
BF = jnp.bfloat16
F32 = jnp.float32
CAP = 3
GROUPS = 4
FLOWS = (
    (2, 0, 256, "z"),
    (3, 0, 128, "y"),
    (0, 0, 256, "y"),
    (1, 0, 128, "x"),
    (1, 128, 128, "z"),
    (3, 128, 128, "y"),
)
SPLIT = (9, 10, 13, 16, 2, 3, 6, 19, 20, 23, 26)


def dot_nt(a, b):
    return lax.dot_general(a, b, (((1,), (1,)), ((), ())), preferred_element_type=F32)


def dot_nn(a, b):
    return lax.dot_general(a, b, (((1,), (0,)), ((), ())), preferred_element_type=F32)


def kernel(
    scale, links, routes, g_hbm, p_hbm, w_hbm, dw_hbm, fine_hbm,
    fg, conv, down_out,
    g, p, face, pface, gsh, ash, gt, w, dw, fine, acc, octs, out, octin, ot,
    part, rcore, racc, r1, a1, r2, red,
    load_sem, halo_s, halo_r, oct_s, oct_r, red_s, red_r,
):
    dp = lax.axis_index("dp")
    dom = lax.axis_index("dom")
    zc, cc = dp // 2, dp % 2
    yc, xc = dom // 4, dom % 4
    coord = {"z": zc, "x": xc, "y": yc}

    def at_offset(**offsets):
        z, x, y = (lax.rem(coord[a] + offsets.get(a, 0), 4) for a in "zxy")
        return (z * 2 + cc, y * 4 + x)

    partner = (zc * 2 + (1 - cc), dom)
    nxt = (dp, lax.rem(dom + 1, 16))
    prv = (dp, lax.rem(dom + 15, 16))

    barrier = pltpu.get_barrier_semaphore()
    peers = [partner, nxt, prv]
    for z in range(4):
        for x in range(4):
            for y in range(4):
                if (z, x, y) != (0, 0, 0) and 0 in (z, x, y):
                    peers.append(at_offset(z=z, x=x, y=y))
    for peer in peers:
        pl.semaphore_signal(barrier, inc=1, device_id=peer, device_id_type=MESH)

    loads = []
    for i, (src, dst) in enumerate(
        ((g_hbm, g.at[0:CAP]), (p_hbm, p.at[0:CAP]), (w_hbm, w), (fine_hbm, fine), (dw_hbm, dw))
    ):
        c = pltpu.make_async_copy(src, dst, load_sem.at[i])
        c.start()
        loads.append(c)
    g[CAP] = jnp.zeros(g.shape[1:], BF)
    p[CAP] = jnp.zeros(p.shape[1:], BF)
    for i in range(2):
        face[i, CAP] = jnp.zeros(face.shape[2:], BF)
        pface[i, CAP] = jnp.zeros(face.shape[2:], BF)
    octs[24] = jnp.zeros(octs.shape[1:], BF)
    for s in range(8):
        part[3, s // 2, s % 2, 3, :, :, 0:128] = jnp.zeros((4, 16, 128), BF)
    loads[0].wait()
    loads[1].wait()

    def rcopy(src, dst, ss, rs, to):
        return pltpu.make_async_remote_copy(
            src_ref=src, dst_ref=dst, send_sem=ss, recv_sem=rs, device_id=to, device_id_type=MESH
        )

    zi = lax.broadcasted_iota(jnp.int32, (10, 8, 256), 1)

    def expand(load, a, blk, plane, dst, relu):
        def slot(b, c):
            n = links[blk, 0, 9 * (a + 1) + 3 * (b + 1) + (c + 1)]
            return jnp.where(n < 0, CAP, n)

        cols = []
        for c in (-1, 0, 1):
            low = load(slot(-1, c), pl.ds(48, 16)).astype(F32)[8:16]
            mid = load(slot(0, c), pl.ds(0, 64)).astype(F32)
            high = load(slot(1, c), pl.ds(0, 16)).astype(F32)[0:8]
            col = jnp.concatenate([low, mid, high], axis=0)
            if relu:
                col = jnp.maximum(col, 0.0)
            cols.append(col.reshape(10, 8, 256))
        shifted = (
            pltpu.roll(jnp.where(zi == 7, cols[0], cols[1]), 1, 1),
            cols[1],
            pltpu.roll(jnp.where(zi == 0, cols[2], cols[1]), 7, 1),
        )
        rows = pl.ds(pl.multiple_of(blk * 64, 64), 64)
        for ty in range(3):
            for tz in range(3):
                dst[3 * ty + tz, plane, rows] = shifted[tz][ty : ty + 8].reshape(64, 256).astype(BF)

    def inner_g(n, _):
        blk, x = n // 8, n % 8
        expand(lambda s, r: g[s, x, r], 0, blk, x + 1, gsh, False)
        return 0

    def outer_g(blk, _):
        expand(lambda s, r: face[0, s, r], -1, blk, 0, gsh, False)
        expand(lambda s, r: face[1, s, r], 1, blk, 9, gsh, False)
        return 0

    def inner_p(n, _):
        blk, x = n // 8, n % 8
        expand(lambda s, r: p[s, x, r], 0, blk, x + 1, ash, True)
        return 0

    def outer_p(blk, _):
        expand(lambda s, r: pface[0, s, r], -1, blk, 0, ash, True)
        expand(lambda s, r: pface[1, s, r], 1, blk, 9, ash, True)
        return 0

    def input_grad(half, first, last):
        def taps(tx, _):
            rows = pl.ds(2 - tx + 4 * half, 4)
            lhs = jnp.concatenate([gsh[8 - n, rows].reshape(768, 256) for n in range(9)], axis=1)
            rhs = jnp.concatenate([w[9 * tx + n] for n in range(9)], axis=1)
            acc[half] += dot_nt(lhs, rhs)
            return 0

        lax.fori_loop(first, last, taps, 0)

    lower = lax.broadcasted_iota(jnp.int32, (2, 8, 256), 1) < 4

    def octants(half):
        def plane(n, _):
            cx, blk = n // CAP, n % CAP
            val = acc[half, pl.ds(pl.multiple_of(n * 64, 64), 64)]
            pre = p[blk, 4 * half + cx].astype(F32)
            val = jnp.where(pre > 0.0, val, 0.0).reshape(2, 2, 2, 8, 256)
            for oy in range(2):
                even, odd = val[oy, :, 0], val[oy, :, 1]
                first = jnp.where(lower, even, pltpu.roll(odd, 4, 1))
                second = jnp.where(lower, pltpu.roll(even, 4, 1), odd)
                rows = pl.ds(pl.multiple_of(cx * 16, 16), 16)
                slot = blk * 8 + 4 * half + 2 * oy
                octs[slot, rows] = first.reshape(16, 256).astype(BF)
                octs[slot + 1, rows] = second.reshape(16, 256).astype(BF)
            return 0

        lax.fori_loop(0, 4 * CAP, plane, 0)

    passing = []

    def route(half):
        def place(k):
            def one(j, _):
                e = routes[0, k, 0, j]
                val = octs[jnp.where(e < 0, 24, e)]
                if k == 1:
                    octin[8 + j] = val
                else:
                    out[k // 2, j] = val
                return 0

            lax.fori_loop(4 * half, 4 * half + 4, one, 0)

        place(0)
        place(2)
        for k, base, to in ((0, 0, prv), (1, 16, nxt)):
            i = 2 * half + k
            c = rcopy(
                out.at[k, 4 * half : 4 * half + 4],
                octin.at[base + 4 * half : base + 4 * half + 4],
                oct_s.at[i], oct_r.at[i], to,
            )
            c.start()
            passing.append(c)
        place(1)

    lax.fori_loop(0, CAP * 8, inner_p, 0)
    pl.semaphore_wait(barrier, len(peers))

    halos = []
    for i, (src, dst, to) in enumerate(
        (
            (p.at[0:CAP, 7], pface.at[0], nxt),
            (p.at[0:CAP, 0], pface.at[1], prv),
            (g.at[0:CAP, 7], face.at[0], nxt),
            (g.at[0:CAP, 0], face.at[1], prv),
        )
    ):
        c = rcopy(src, dst.at[0:CAP], halo_s.at[i], halo_r.at[i], to)
        c.start()
        halos.append(c)

    lax.fori_loop(0, CAP * 8, inner_g, 0)
    acc[...] = jnp.zeros(acc.shape, F32)

    def transpose_plane(x, _):
        gt[:, pl.ds(pl.multiple_of(x * 384, 384), 384)] = (
            gsh[4, pl.ds(1 + 2 * x, 2)].reshape(384, 256).T
        )
        return 0

    lax.fori_loop(0, 4, transpose_plane, 0)

    def tap(t):
        tx, tyz = t // 9, t % 9
        rows = ash[tyz, pl.ds(tx, 8)].reshape(1536, 256)
        return dot_nn(gt[...], rows).T.astype(BF)

    def whole_tap(shift):
        def one(z, _):
            rows = []
            for c in range(2):
                t = (27 * (2 * z + c) + 7) // 8 + shift
                rows.append(ash[t % 9, pl.ds(t // 9, 8)].reshape(1536, 256))
            grad = dot_nn(gt[...], jnp.concatenate(rows, axis=1)).T.astype(BF)
            part[shift, z] = grad.reshape(2, 4, 4, 16, 256)
            return 0

        return one

    def split_tap(t):
        grad = tap(t)
        for i in range(8):
            k, r = divmod(8 * t + i, 27)
            pos = r if t < (27 * k + 7) // 8 else r - 16
            rows = grad[32 * i : 32 * i + 32]
            if pos < 8:
                y = pos % 2 * 2
                part[2, k // 2, k % 2, pos // 2, y : y + 2] = rows.reshape(2, 16, 256)
            else:
                for n in range(4):
                    part[3, k // 2, k % 2, pos - 8, n, :, 0:128] = rows[
                        n // 2 * 16 : n // 2 * 16 + 16, n % 2 * 128 : n % 2 * 128 + 128
                    ]

    def cut(ref, axis, at):
        return ref.at[tuple(at if d == axis else slice(None) for d in "zxy")]

    class Flow:
        def __init__(self, n):
            self.n = n
            grp, lane, width, self.axis = FLOWS[n]
            lanes = pl.ds(lane, width)
            self.part = part.at[grp, :, :, :, :, :, lanes]
            self.rcore = rcore.at[grp, :, :, :, :, lanes]
            self.racc = racc.at[grp, :, :, :, :, lanes]
            self.r1 = r1.at[grp, :, :, :, :, lanes]
            self.a1 = a1.at[grp, :, :, :, lanes]
            self.r2 = r2.at[grp, :, :, lanes]
            self.red = red.at[grp, :, :, :, lanes]
            self.stage = 0

        def send(self, src, dst, i, to):
            c = rcopy(src, dst, red_s.at[self.n, i], red_r.at[self.n, i], to)
            c.start()
            return c

        def all_of(self, i):
            ref = (self.rcore, self.r1, self.r2, self.r2)[i]
            return rcopy(ref, ref, red_s.at[self.n, i], red_r.at[self.n, i], partner)

        def chunk(self, off):
            return cut(self.racc, self.axis, lax.rem(coord[self.axis] + off, 4))

        def step(self):
            axis = self.axis
            u, v = "zxy".replace(axis, "")
            stage = self.stage
            self.stage += 1
            if stage > 0:
                self.all_of(stage - 1).wait_recv()
            if stage == 0:
                self.send(self.part.at[:, 1 - cc], self.rcore, 0, partner)
            elif stage == 1:
                for z in range(4):
                    self.racc[z] = (
                        self.part[z, cc].astype(F32) + self.rcore[z].astype(F32)
                    ).astype(BF)
                for off in (2, 1, 3):
                    self.send(self.chunk(off), self.r1.at[off - 1], 1, at_offset(**{axis: off}))
            elif stage == 2:
                total = self.chunk(0)[...].astype(F32)
                for n in range(3):
                    total = total + self.r1[n].astype(F32)
                self.a1[...] = total.astype(BF)
                for n in range(1, 16):
                    du, dv = n // 4, n % 4
                    src = self.a1.at[lax.rem(coord[u] + du, 4), lax.rem(coord[v] + dv, 4)]
                    self.send(src, self.r2.at[n - 1], 2, at_offset(**{u: du, v: dv}))
            elif stage == 3:
                total = self.a1[coord[u], coord[v]].astype(F32)
                for n in range(15):
                    total = total + self.r2[n].astype(F32)
                self.red[xc, yc] = total.astype(BF)
                spot = self.red.at[xc, yc]
                for n in range(1, 16):
                    self.send(spot, spot, 3, at_offset(x=n // 4, y=n % 4))

        def finish(self):
            for i in range(4):
                self.all_of(i).wait_send()

    flows = [Flow(i) for i in range(len(FLOWS))]
    fc, fa, fb, fd = flows[0:2], flows[2:3], flows[3:5], flows[5:6]

    def step(*some):
        for group in some:
            for one in group:
                one.step()

    for t in SPLIT[:4]:
        split_tap(t)
    halos[0].wait_recv()
    halos[1].wait_recv()
    lax.fori_loop(0, CAP, outer_p, 0)
    for t in SPLIT[4:]:
        split_tap(t)
    step(fc)
    lax.fori_loop(0, 4, whole_tap(0), 0)
    step(fa)
    halos[2].wait_recv()
    halos[3].wait_recv()
    lax.fori_loop(0, CAP, outer_g, 0)
    loads[2].wait()
    input_grad(0, 0, 2)
    step(fc)
    input_grad(0, 2, 3)
    step(fa)
    octants(0)
    route(0)
    input_grad(1, 0, 3)
    octants(1)
    route(1)
    lax.fori_loop(0, 4, whole_tap(1), 0)
    step(fb)
    loads[4].wait()

    def fine_grad(i, _):
        at = pl.ds(4 * i, 4)
        res = dot_nt(octin[at].reshape(256, 256), dw[...]).astype(BF)
        for q in range(8):
            fg[at, q] = res[:, 128 * q : 128 * q + 128].reshape(4, 64, 128)
        return 0

    lax.fori_loop(2, 4, fine_grad, 0)
    loads[3].wait()
    for c in passing:
        c.wait_recv()
    step(fb)

    def turn(i, _):
        ot[:, pl.ds(pl.multiple_of(i * 384, 384), 384)] = (
            octin[pl.ds(6 * i, 6)].reshape(384, 256).T
        )
        return 0

    lax.fori_loop(0, 4, turn, 0)

    def down(i, _):
        rows = jnp.concatenate(
            [fine[:, 2 * i].reshape(1536, 128), fine[:, 2 * i + 1].reshape(1536, 128)], axis=1
        )
        grad = dot_nn(ot[...], rows).T.astype(BF)
        for c in range(2):
            one = grad[128 * c : 128 * c + 128]
            for n in range(16):
                part[3, i, c, n // 4, n % 4, :, 128:256] = one[
                    n // 2 * 16 : n // 2 * 16 + 16, n % 2 * 128 : n % 2 * 128 + 128
                ]
        return 0

    lax.fori_loop(0, 4, down, 0)
    step(fd, fc, fa)
    lax.fori_loop(0, 2, fine_grad, 0)
    lax.fori_loop(4, 6, fine_grad, 0)
    step(fd, fb)

    lead = (27 * dp + 7) // 8 * 8 - 27 * dp
    start = pl.multiple_of(lead * 32, 32)

    def finished(value):
        return value.astype(F32) * scale

    step(fc, fa, fd, fb, fc)
    for n in range(11):
        row = pl.multiple_of(32 * (n + jnp.where(n < lead, 0, 16)), 32)
        if n < 8:
            piece = red[2, n // 2, (n % 2) * 2 : (n % 2) * 2 + 2]
            conv[pl.ds(row, 32)] = finished(piece.reshape(32, 256))
        else:
            for m in range(4):
                conv[pl.ds(row + m // 2 * 16, 16), m % 2 * 128 : m % 2 * 128 + 128] = finished(
                    red[3, n - 8, m, :, 0:128]
                )
    step(fa)
    conv[pl.ds(start, 256)] = finished(red[0].reshape(256, 256))
    step(fd, fb)
    conv[pl.ds(start + 256, 256)] = finished(red[1].reshape(256, 256))
    step(fd)
    for n in range(16):
        down_out[n // 2 * 16 : n // 2 * 16 + 16, n % 2 * 128 : n % 2 * 128 + 128] = finished(
            red[3, n // 4, n % 4, :, 128:256]
        )
    for c in halos + passing:
        c.wait_send()
    for one in flows:
        one.finish()


def body(grad_out, pre_act, conv_weight, down_weight, fine_act, neighbours, octant_routes):
    slots, voxels, channels = grad_out.shape[1:]
    any_space = pl.BlockSpec(memory_space=pl.ANY)
    smem = pl.BlockSpec(memory_space=pltpu.SMEM)
    V = pltpu.VMEM
    factor = 1.0 / math.sqrt(lax.axis_size("dp") * lax.axis_size("dom") * slots * voxels)
    vmem = pl.BlockSpec(memory_space=V)
    fg, conv, down = pl.pallas_call(
        functools.partial(kernel, factor),
        out_shape=(V((24, 8, 64, 128), BF), V((864, 256), F32), V((128, 256), F32)),
        in_specs=[smem, smem] + [any_space] * 5,
        out_specs=(vmem, vmem, vmem),
        scratch_shapes=[
            V((CAP + 1, 8, 64, 256), BF),
            V((CAP + 1, 8, 64, 256), BF),
            V((2, CAP + 1, 64, 256), BF),
            V((2, CAP + 1, 64, 256), BF),
            V((9, 10, 192, 256), BF),
            V((9, 10, 192, 256), BF),
            V((256, 1536), BF),
            V((27, 256, 256), BF),
            V((1024, 256), BF),
            V((24, 8, 64, 128), BF),
            V((2, 768, 256), F32),
            V((25, 64, 256), BF),
            V((2, 8, 64, 256), BF),
            V((24, 64, 256), BF),
            V((256, 1536), BF),
            V((GROUPS, 4, 2, 4, 4, 16, 256), BF),
            V((GROUPS, 4, 4, 4, 16, 256), BF),
            V((GROUPS, 4, 4, 4, 16, 256), BF),
            V((GROUPS, 3, 4, 4, 16, 256), BF),
            V((GROUPS, 4, 4, 16, 256), BF),
            V((GROUPS, 15, 16, 256), BF),
            V((GROUPS, 4, 4, 16, 256), BF),
            pltpu.SemaphoreType.DMA((5,)),
            pltpu.SemaphoreType.DMA((4,)),
            pltpu.SemaphoreType.DMA((4,)),
            pltpu.SemaphoreType.DMA((4,)),
            pltpu.SemaphoreType.DMA((4,)),
            pltpu.SemaphoreType.DMA((len(FLOWS), 4)),
            pltpu.SemaphoreType.DMA((len(FLOWS), 4)),
        ],
        compiler_params=pltpu.CompilerParams(
            collective_id=0, has_side_effects=True, vmem_limit_bytes=54 * 1024 * 1024
        ),
        name="backward",
    )(
        neighbours.transpose(1, 0, 2),
        octant_routes.transpose(0, 2, 1, 3),
        grad_out[0].reshape(slots, 8, 64, channels),
        pre_act[0].reshape(slots, 8, 64, channels),
        conv_weight,
        down_weight.reshape(1024, 256),
        fine_act[0].reshape(24, 8, 64, 128),
    )
    return (fg.reshape(fine_act.shape), conv, down)


def solution(mesh):
    return jax.shard_map(
        body,
        mesh=mesh,
        in_specs=(
            P("dp", "dom", None, None),
            P("dp", "dom", None, None),
            P(),
            P(),
            P("dp", "dom", None, None),
            P("dp", "dom", None),
            P("dp", "dom", None, None),
        ),
        out_specs=(P("dp", "dom", None, None), P("dp", None), P("dp", None)),
        check_vma=False,
    )
```

```python
import functools
import math

import jax
import jax.numpy as jnp
from jax import lax
from jax.experimental import pallas as pl
from jax.experimental.pallas import tpu as pltpu
from jax.sharding import PartitionSpec as P

MESH = pl.DeviceIdType.MESH
BF = jnp.bfloat16
F32 = jnp.float32
CAP = 3
GROUPS = 4
FLOWS = (
    (2, 0, 256, "z"),
    (3, 0, 128, "y"),
    (0, 0, 256, "y"),
    (1, 0, 128, "x"),
    (1, 128, 128, "z"),
    (3, 128, 128, "y"),
)
FAR = sorted(range(1, 16), key=lambda n: -(min(n // 4, 4 - n // 4) + min(n % 4, 4 - n % 4)))
SPLIT = (9, 10, 13, 16, 2, 3, 6, 19, 20, 23, 26)


def dot_nt(a, b):
    return lax.dot_general(a, b, (((1,), (1,)), ((), ())), preferred_element_type=F32)


def dot_nn(a, b):
    return lax.dot_general(a, b, (((1,), (0,)), ((), ())), preferred_element_type=F32)


def kernel(
    scale, links, routes, g_hbm, p_hbm, w_hbm, dw_hbm, fine_hbm,
    fg, conv, down_out,
    g, p, face, pface, gsh, ash, gt, w, dw, fine, acc, octs, out, octin, ot,
    part, rcore, racc, r1, a1, r2, red,
    load_sem, halo_s, halo_r, oct_s, oct_r, red_s, red_r,
):
    dp = lax.axis_index("dp")
    dom = lax.axis_index("dom")
    zc, cc = dp // 2, dp % 2
    yc, xc = dom // 4, dom % 4
    coord = {"z": zc, "x": xc, "y": yc}

    def at_offset(**offsets):
        z, x, y = (lax.rem(coord[a] + offsets.get(a, 0), 4) for a in "zxy")
        return (z * 2 + cc, y * 4 + x)

    partner = (zc * 2 + (1 - cc), dom)
    nxt = (dp, lax.rem(dom + 1, 16))
    prv = (dp, lax.rem(dom + 15, 16))

    barrier = pltpu.get_barrier_semaphore()
    peers = [partner, nxt, prv]
    for z in range(4):
        for x in range(4):
            for y in range(4):
                if (z, x, y) != (0, 0, 0) and 0 in (z, x, y):
                    peers.append(at_offset(z=z, x=x, y=y))
    for peer in peers:
        pl.semaphore_signal(barrier, inc=1, device_id=peer, device_id_type=MESH)

    loads = []
    for i, (src, dst) in enumerate(
        ((g_hbm, g.at[0:CAP]), (p_hbm, p.at[0:CAP]), (w_hbm, w), (fine_hbm, fine), (dw_hbm, dw))
    ):
        c = pltpu.make_async_copy(src, dst, load_sem.at[i])
        c.start()
        loads.append(c)
    g[CAP] = jnp.zeros(g.shape[1:], BF)
    p[CAP] = jnp.zeros(p.shape[1:], BF)
    for i in range(2):
        face[i, CAP] = jnp.zeros(face.shape[2:], BF)
        pface[i, CAP] = jnp.zeros(face.shape[2:], BF)
    octs[24] = jnp.zeros(octs.shape[1:], BF)
    for s in range(8):
        part[3, s // 2, s % 2, 3, :, :, 0:128] = jnp.zeros((4, 16, 128), BF)
    loads[0].wait()
    loads[1].wait()

    def rcopy(src, dst, ss, rs, to):
        return pltpu.make_async_remote_copy(
            src_ref=src, dst_ref=dst, send_sem=ss, recv_sem=rs, device_id=to, device_id_type=MESH
        )

    zi = lax.broadcasted_iota(jnp.int32, (10, 8, 256), 1)

    def expand(load, a, blk, plane, dst, relu):
        def slot(b, c):
            n = links[blk, 0, 9 * (a + 1) + 3 * (b + 1) + (c + 1)]
            return jnp.where(n < 0, CAP, n)

        cols = []
        for c in (-1, 0, 1):
            low = load(slot(-1, c), pl.ds(48, 16)).astype(F32)[8:16]
            mid = load(slot(0, c), pl.ds(0, 64)).astype(F32)
            high = load(slot(1, c), pl.ds(0, 16)).astype(F32)[0:8]
            col = jnp.concatenate([low, mid, high], axis=0)
            if relu:
                col = jnp.maximum(col, 0.0)
            cols.append(col.reshape(10, 8, 256))
        shifted = (
            pltpu.roll(jnp.where(zi == 7, cols[0], cols[1]), 1, 1),
            cols[1],
            pltpu.roll(jnp.where(zi == 0, cols[2], cols[1]), 7, 1),
        )
        rows = pl.ds(pl.multiple_of(blk * 64, 64), 64)
        for ty in range(3):
            for tz in range(3):
                dst[3 * ty + tz, plane, rows] = shifted[tz][ty : ty + 8].reshape(64, 256).astype(BF)

    def inner_g(n, _):
        blk, x = n // 8, n % 8
        expand(lambda s, r: g[s, x, r], 0, blk, x + 1, gsh, False)
        return 0

    def outer_g(blk, _):
        expand(lambda s, r: face[0, s, r], -1, blk, 0, gsh, False)
        expand(lambda s, r: face[1, s, r], 1, blk, 9, gsh, False)
        return 0

    def inner_p(n, _):
        blk, x = n // 8, n % 8
        expand(lambda s, r: p[s, x, r], 0, blk, x + 1, ash, True)
        return 0

    def outer_p(blk, _):
        expand(lambda s, r: pface[0, s, r], -1, blk, 0, ash, True)
        expand(lambda s, r: pface[1, s, r], 1, blk, 9, ash, True)
        return 0

    def input_grad(half, first, last):
        def taps(tx, _):
            rows = pl.ds(2 - tx + 4 * half, 4)
            lhs = jnp.concatenate([gsh[8 - n, rows].reshape(768, 256) for n in range(9)], axis=1)
            rhs = jnp.concatenate([w[9 * tx + n] for n in range(9)], axis=1)
            acc[half] += dot_nt(lhs, rhs)
            return 0

        lax.fori_loop(first, last, taps, 0)

    lower = lax.broadcasted_iota(jnp.int32, (2, 8, 256), 1) < 4

    def octants(half):
        def plane(n, _):
            cx, blk = n // CAP, n % CAP
            val = acc[half, pl.ds(pl.multiple_of(n * 64, 64), 64)]
            pre = p[blk, 4 * half + cx].astype(F32)
            val = jnp.where(pre > 0.0, val, 0.0).reshape(2, 2, 2, 8, 256)
            for oy in range(2):
                even, odd = val[oy, :, 0], val[oy, :, 1]
                first = jnp.where(lower, even, pltpu.roll(odd, 4, 1))
                second = jnp.where(lower, pltpu.roll(even, 4, 1), odd)
                rows = pl.ds(pl.multiple_of(cx * 16, 16), 16)
                slot = blk * 8 + 4 * half + 2 * oy
                octs[slot, rows] = first.reshape(16, 256).astype(BF)
                octs[slot + 1, rows] = second.reshape(16, 256).astype(BF)
            return 0

        lax.fori_loop(0, 4 * CAP, plane, 0)

    passing = []

    def route(half):
        def place(k):
            def one(j, _):
                e = routes[0, k, 0, j]
                val = octs[jnp.where(e < 0, 24, e)]
                if k == 1:
                    octin[8 + j] = val
                else:
                    out[k // 2, j] = val
                return 0

            lax.fori_loop(4 * half, 4 * half + 4, one, 0)

        place(0)
        place(2)
        for k, base, to in ((0, 0, prv), (1, 16, nxt)):
            i = 2 * half + k
            c = rcopy(
                out.at[k, 4 * half : 4 * half + 4],
                octin.at[base + 4 * half : base + 4 * half + 4],
                oct_s.at[i], oct_r.at[i], to,
            )
            c.start()
            passing.append(c)
        place(1)

    lax.fori_loop(0, CAP * 8, inner_p, 0)
    pl.semaphore_wait(barrier, len(peers))

    halos = []
    for i, (src, dst, to) in enumerate(
        (
            (p.at[0:CAP, 7], pface.at[0], nxt),
            (p.at[0:CAP, 0], pface.at[1], prv),
            (g.at[0:CAP, 7], face.at[0], nxt),
            (g.at[0:CAP, 0], face.at[1], prv),
        )
    ):
        c = rcopy(src, dst.at[0:CAP], halo_s.at[i], halo_r.at[i], to)
        c.start()
        halos.append(c)

    lax.fori_loop(0, CAP * 8, inner_g, 0)
    acc[...] = jnp.zeros(acc.shape, F32)

    def transpose_plane(x, _):
        gt[:, pl.ds(pl.multiple_of(x * 384, 384), 384)] = (
            gsh[4, pl.ds(1 + 2 * x, 2)].reshape(384, 256).T
        )
        return 0

    lax.fori_loop(0, 4, transpose_plane, 0)

    def tap(t):
        tx, tyz = t // 9, t % 9
        rows = ash[tyz, pl.ds(tx, 8)].reshape(1536, 256)
        return dot_nn(gt[...], rows).T.astype(BF)

    def whole_tap(shift):
        def one(z, _):
            rows = []
            for c in range(2):
                t = (27 * (2 * z + c) + 7) // 8 + shift
                rows.append(ash[t % 9, pl.ds(t // 9, 8)].reshape(1536, 256))
            grad = dot_nn(gt[...], jnp.concatenate(rows, axis=1)).T.astype(BF)
            part[shift, z] = grad.reshape(2, 4, 4, 16, 256)
            return 0

        return one

    def split_tap(t):
        grad = tap(t)
        for i in range(8):
            k, r = divmod(8 * t + i, 27)
            pos = r if t < (27 * k + 7) // 8 else r - 16
            rows = grad[32 * i : 32 * i + 32]
            if pos < 8:
                y = pos % 2 * 2
                part[2, k // 2, k % 2, pos // 2, y : y + 2] = rows.reshape(2, 16, 256)
            else:
                for n in range(4):
                    part[3, k // 2, k % 2, pos - 8, n, :, 0:128] = rows[
                        n // 2 * 16 : n // 2 * 16 + 16, n % 2 * 128 : n % 2 * 128 + 128
                    ]

    def cut(ref, axis, at):
        return ref.at[tuple(at if d == axis else slice(None) for d in "zxy")]

    class Flow:
        def __init__(self, n):
            self.n = n
            grp, lane, width, self.axis = FLOWS[n]
            lanes = pl.ds(lane, width)
            self.part = part.at[grp, :, :, :, :, :, lanes]
            self.rcore = rcore.at[grp, :, :, :, :, lanes]
            self.racc = racc.at[grp, :, :, :, :, lanes]
            self.r1 = r1.at[grp, :, :, :, :, lanes]
            self.a1 = a1.at[grp, :, :, :, lanes]
            self.r2 = r2.at[grp, :, :, lanes]
            self.red = red.at[grp, :, :, :, lanes]
            self.stage = 0

        def send(self, src, dst, i, to):
            c = rcopy(src, dst, red_s.at[self.n, i], red_r.at[self.n, i], to)
            c.start()
            return c

        def all_of(self, i):
            ref = (self.rcore, self.r1, self.r2, self.r2)[i]
            return rcopy(ref, ref, red_s.at[self.n, i], red_r.at[self.n, i], partner)

        def chunk(self, off):
            return cut(self.racc, self.axis, lax.rem(coord[self.axis] + off, 4))

        def step(self):
            axis = self.axis
            u, v = "zxy".replace(axis, "")
            stage = self.stage
            self.stage += 1
            if stage > 0:
                self.all_of(stage - 1).wait_recv()
            if stage == 0:
                self.send(self.part.at[:, 1 - cc], self.rcore, 0, partner)
            elif stage == 1:
                for z in range(4):
                    self.racc[z] = (
                        self.part[z, cc].astype(F32) + self.rcore[z].astype(F32)
                    ).astype(BF)
                for off in (2, 1, 3):
                    self.send(self.chunk(off), self.r1.at[off - 1], 1, at_offset(**{axis: off}))
            elif stage == 2:
                total = self.chunk(0)[...].astype(F32)
                for n in range(3):
                    total = total + self.r1[n].astype(F32)
                self.a1[...] = total.astype(BF)
                for n in FAR:
                    du, dv = n // 4, n % 4
                    src = self.a1.at[lax.rem(coord[u] + du, 4), lax.rem(coord[v] + dv, 4)]
                    self.send(src, self.r2.at[n - 1], 2, at_offset(**{u: du, v: dv}))
            elif stage == 3:
                total = self.a1[coord[u], coord[v]].astype(F32)
                for n in range(15):
                    total = total + self.r2[n].astype(F32)
                self.red[xc, yc] = total.astype(BF)
                spot = self.red.at[xc, yc]
                for n in FAR:
                    self.send(spot, spot, 3, at_offset(x=n // 4, y=n % 4))

        def finish(self):
            for i in range(4):
                self.all_of(i).wait_send()

    flows = [Flow(i) for i in range(len(FLOWS))]
    fc, fa, fb, fd = flows[0:2], flows[2:3], flows[3:5], flows[5:6]

    def step(*some):
        for group in some:
            for one in group:
                one.step()

    for t in SPLIT[:4]:
        split_tap(t)
    halos[0].wait_recv()
    halos[1].wait_recv()
    lax.fori_loop(0, CAP, outer_p, 0)
    for t in SPLIT[4:]:
        split_tap(t)
    step(fc)
    lax.fori_loop(0, 4, whole_tap(0), 0)
    step(fa)
    halos[2].wait_recv()
    halos[3].wait_recv()
    lax.fori_loop(0, CAP, outer_g, 0)
    loads[2].wait()
    input_grad(0, 0, 2)
    step(fc)
    input_grad(0, 2, 3)
    step(fa)
    octants(0)
    route(0)
    input_grad(1, 0, 3)
    octants(1)
    route(1)
    lax.fori_loop(0, 4, whole_tap(1), 0)
    step(fb)
    loads[4].wait()

    def fine_grad(i, _):
        at = pl.ds(4 * i, 4)
        res = dot_nt(octin[at].reshape(256, 256), dw[...]).astype(BF)
        for q in range(8):
            fg[at, q] = res[:, 128 * q : 128 * q + 128].reshape(4, 64, 128)
        return 0

    lax.fori_loop(2, 4, fine_grad, 0)
    loads[3].wait()
    for c in passing:
        c.wait_recv()
    step(fb)

    def turn(i, _):
        ot[:, pl.ds(pl.multiple_of(i * 384, 384), 384)] = (
            octin[pl.ds(6 * i, 6)].reshape(384, 256).T
        )
        return 0

    lax.fori_loop(0, 4, turn, 0)

    def down(i, _):
        rows = jnp.concatenate(
            [fine[:, 2 * i].reshape(1536, 128), fine[:, 2 * i + 1].reshape(1536, 128)], axis=1
        )
        grad = dot_nn(ot[...], rows).T.astype(BF)
        for c in range(2):
            one = grad[128 * c : 128 * c + 128]
            for n in range(16):
                part[3, i, c, n // 4, n % 4, :, 128:256] = one[
                    n // 2 * 16 : n // 2 * 16 + 16, n % 2 * 128 : n % 2 * 128 + 128
                ]
        return 0

    lax.fori_loop(0, 4, down, 0)
    step(fd, fc, fa)
    lax.fori_loop(0, 2, fine_grad, 0)
    lax.fori_loop(4, 6, fine_grad, 0)
    step(fd, fb)

    lead = (27 * dp + 7) // 8 * 8 - 27 * dp
    start = pl.multiple_of(lead * 32, 32)

    def finished(value):
        return value.astype(F32) * scale

    step(fc, fa, fd, fb, fc)
    for n in range(11):
        row = pl.multiple_of(32 * (n + jnp.where(n < lead, 0, 16)), 32)
        if n < 8:
            piece = red[2, n // 2, (n % 2) * 2 : (n % 2) * 2 + 2]
            conv[pl.ds(row, 32)] = finished(piece.reshape(32, 256))
        else:
            for m in range(4):
                conv[pl.ds(row + m // 2 * 16, 16), m % 2 * 128 : m % 2 * 128 + 128] = finished(
                    red[3, n - 8, m, :, 0:128]
                )
    step(fa)
    conv[pl.ds(start, 256)] = finished(red[0].reshape(256, 256))
    step(fd, fb)
    conv[pl.ds(start + 256, 256)] = finished(red[1].reshape(256, 256))
    step(fd)
    for n in range(16):
        down_out[n // 2 * 16 : n // 2 * 16 + 16, n % 2 * 128 : n % 2 * 128 + 128] = finished(
            red[3, n // 4, n % 4, :, 128:256]
        )
    for c in halos + passing:
        c.wait_send()
    for one in flows:
        one.finish()


def body(grad_out, pre_act, conv_weight, down_weight, fine_act, neighbours, octant_routes):
    slots, voxels, channels = grad_out.shape[1:]
    any_space = pl.BlockSpec(memory_space=pl.ANY)
    smem = pl.BlockSpec(memory_space=pltpu.SMEM)
    V = pltpu.VMEM
    factor = 1.0 / math.sqrt(lax.axis_size("dp") * lax.axis_size("dom") * slots * voxels)
    vmem = pl.BlockSpec(memory_space=V)
    fg, conv, down = pl.pallas_call(
        functools.partial(kernel, factor),
        out_shape=(V((24, 8, 64, 128), BF), V((864, 256), F32), V((128, 256), F32)),
        in_specs=[smem, smem] + [any_space] * 5,
        out_specs=(vmem, vmem, vmem),
        scratch_shapes=[
            V((CAP + 1, 8, 64, 256), BF),
            V((CAP + 1, 8, 64, 256), BF),
            V((2, CAP + 1, 64, 256), BF),
            V((2, CAP + 1, 64, 256), BF),
            V((9, 10, 192, 256), BF),
            V((9, 10, 192, 256), BF),
            V((256, 1536), BF),
            V((27, 256, 256), BF),
            V((1024, 256), BF),
            V((24, 8, 64, 128), BF),
            V((2, 768, 256), F32),
            V((25, 64, 256), BF),
            V((2, 8, 64, 256), BF),
            V((24, 64, 256), BF),
            V((256, 1536), BF),
            V((GROUPS, 4, 2, 4, 4, 16, 256), BF),
            V((GROUPS, 4, 4, 4, 16, 256), BF),
            V((GROUPS, 4, 4, 4, 16, 256), BF),
            V((GROUPS, 3, 4, 4, 16, 256), BF),
            V((GROUPS, 4, 4, 16, 256), BF),
            V((GROUPS, 15, 16, 256), BF),
            V((GROUPS, 4, 4, 16, 256), BF),
            pltpu.SemaphoreType.DMA((5,)),
            pltpu.SemaphoreType.DMA((4,)),
            pltpu.SemaphoreType.DMA((4,)),
            pltpu.SemaphoreType.DMA((4,)),
            pltpu.SemaphoreType.DMA((4,)),
            pltpu.SemaphoreType.DMA((len(FLOWS), 4)),
            pltpu.SemaphoreType.DMA((len(FLOWS), 4)),
        ],
        compiler_params=pltpu.CompilerParams(
            collective_id=0, has_side_effects=True, vmem_limit_bytes=54 * 1024 * 1024
        ),
        name="backward",
    )(
        neighbours.transpose(1, 0, 2),
        octant_routes.transpose(0, 2, 1, 3),
        grad_out[0].reshape(slots, 8, 64, channels),
        pre_act[0].reshape(slots, 8, 64, channels),
        conv_weight,
        down_weight.reshape(1024, 256),
        fine_act[0].reshape(24, 8, 64, 128),
    )
    return (fg.reshape(fine_act.shape), conv, down)


def solution(mesh):
    return jax.shard_map(
        body,
        mesh=mesh,
        in_specs=(
            P("dp", "dom", None, None),
            P("dp", "dom", None, None),
            P(),
            P(),
            P("dp", "dom", None, None),
            P("dp", "dom", None),
            P("dp", "dom", None, None),
        ),
        out_specs=(P("dp", "dom", None, None), P("dp", None), P("dp", None)),
        check_vma=False,
    )
```
